32 devices in a mesh: groups: 2 (over x), hop: 16 (over z, y, core).
Axes of the slice: x: 2, y: 2, z: 4, core: 2. Of those that a mesh axis runs over, the one named last changes fastest.
Arguments:
- features: bfloat16 [131072, 384], P(('groups', 'hop')), parts along dimension 0, may hold values from -0.29882812 to 0.29882812
- targets: bfloat16 [131072, 384], P(('groups', 'hop')), parts along dimension 0, may hold values from -6 to 6
- row_index: int32 [32, 2, 3, 512], P(('groups', 'hop')), parts along dimension 0, may hold values from 0 to 4095
- hop_order: int32 [4, 16], P('groups'), parts along dimension 0, may hold values from 0 to 15, each once within a row
- weight_in: float32 [32, 384, 512], P(('groups', 'hop')), parts along dimension 0, may hold values from -0.3125 to 0.3125
- weight_out: float32 [32, 512, 384], P(('groups', 'hop')), parts along dimension 0, may hold values from -0.25 to 0.25
- moment_in: bfloat16 [32, 384, 512], P(('groups', 'hop')), parts along dimension 0, may hold values from -0.119628906 to 0.119628906
- moment_out: bfloat16 [32, 512, 384], P(('groups', 'hop')), parts along dimension 0, may hold values from -0.119628906 to 0.119628906
Outputs:
- new_weight_in: float32 [32, 384, 512], P(('groups', 'hop')), parts along dimension 0
- new_weight_out: float32 [32, 512, 384], P(('groups', 'hop')), parts along dimension 0
- new_moment_in: bfloat16 [32, 384, 512], P(('groups', 'hop')), parts along dimension 0
- new_moment_out: bfloat16 [32, 512, 384], P(('groups', 'hop')), parts along dimension 0
The draws below stay inside these ranges and needn't reach their ends.
There are 2 independent parts, one for each index of `groups`. The reference program is written for one: setup_inputs(seed, part) draws one part's arguments, and reference() takes and returns one part's arrays. A program takes and returns all parts, laid end to end along the dimension named above; each array names one. Nothing has to cross between parts.
Inputs may be any that keep to these rules, and one draw needn't show every extreme that they name: `hop_order`: each row is a permutation of 0 to 15.
All inputs are finite; a program needn't handle non-finite values.
Results may differ from the reference program's by a relative error of at most 0.015.
Values may be sent and summed in bfloat16 or wider, within the bound.
No kernel may reach another device: no remote copies, remote signals or barrier semaphores. Data moves between devices by JAX's collectives and lax.ppermute only.
A program may use at most 64 MiB of HBM per device.

```python
import jax
import jax.numpy as jnp
from jax import lax

D = 384
H = 512
ROWS = 512
STEPS = 3
VISITS = 2
SHARD_ROWS = 4096
MODELS = 16
TOTAL_ROWS = 65536


def place_ends(drawn, rng, least, largest):
    place = [jax.random.randint(jax.random.fold_in(rng, axis), (), 0, length) for axis, length in enumerate(drawn.shape)]
    widest = drawn.shape.index(max(drawn.shape))
    next_to = place[:widest] + [(place[widest] + 1) % drawn.shape[widest]] + place[widest + 1:]
    return drawn.at[tuple(place)].set(least).at[tuple(next_to)].set(largest)


def block_levels(key, extent, split, least, largest):
    gain, own = 1.0, jax.random.fold_in(key, 6)
    for position, shards_of in split:
        heights = jnp.exp(jax.random.uniform(jax.random.fold_in(own, position), (shards_of,), jnp.float32, least / len(split), largest / len(split)))
        gain = gain * jnp.repeat(heights, extent[position] // shards_of).reshape([-1 if axis == position else 1 for axis in range(len(extent))])
    return gain


def normal_values(key, extent, deviation, bound, cuts=(), held_as=jnp.bfloat16):
    result = jax.random.normal(key, extent, jnp.float32) * deviation
    if len(cuts) > 0:
        result = block_levels(key, extent, cuts, -0.22, 0.18) * result
    return jnp.clip(result, min=-bound, max=bound).astype(held_as)


def setup_inputs(seed: int = 0, part: int = 0) -> dict:
    key_list = jax.random.split(jax.random.key(seed), 9)
    part_keys = jax.random.split(jax.random.fold_in(key_list[8], part), 9)
    features = normal_values(part_keys[0], (TOTAL_ROWS, D), 0.1, 0.29882812, ((0, 16),))
    targets = normal_values(part_keys[1], (TOTAL_ROWS, D), 1.0, 6.0, ((0, 16),))
    row_index = place_ends(jax.random.randint(part_keys[2], (MODELS, VISITS, STEPS, ROWS), 0, SHARD_ROWS), jax.random.fold_in(part_keys[2], 1), 0, SHARD_ROWS - 1).astype(jnp.int32)
    hop_order = jax.vmap(lambda own: jax.random.permutation(own, MODELS))(jax.random.split(part_keys[3], VISITS)).reshape((VISITS, MODELS)).astype(jnp.int32)
    weight_in = normal_values(part_keys[4], (MODELS, D, H), D ** -0.5, 0.3125, ((0, 16),), jnp.float32)
    weight_out = normal_values(part_keys[5], (MODELS, H, D), H ** -0.5, 0.25, ((0, 16),), jnp.float32)
    moment_in = normal_values(part_keys[6], (MODELS, D, H), 0.02, 0.119628906, ((0, 16),))
    moment_out = normal_values(part_keys[7], (MODELS, H, D), 0.02, 0.119628906, ((0, 16),))
    return dict(features=features, targets=targets, row_index=row_index, hop_order=hop_order, weight_in=weight_in, weight_out=weight_out, moment_in=moment_in, moment_out=moment_out)


MOMENTUM = 0.9
LEARN_RATE = 0.1


def normal_cdf(values):
    return 0.5 * (1.0 + lax.erf(values * 0.7071067811865476))


def normal_pdf(values):
    return 0.3989422804014327 * jnp.exp(-0.5 * values * values)


def train_step(model, batch_x, batch_y):
    weight_in, weight_out, moment_in, moment_out = model
    cast_in = weight_in.astype(jnp.bfloat16)
    cast_out = weight_out.astype(jnp.bfloat16)
    preact = jnp.dot(batch_x, cast_in, preferred_element_type=jnp.float32)
    hidden = (preact * normal_cdf(preact)).astype(jnp.bfloat16)
    error_rows = batch_x.astype(jnp.float32) + jnp.dot(hidden, cast_out, preferred_element_type=jnp.float32) - batch_y.astype(jnp.float32)
    d_out = (error_rows / batch_x.shape[0]).astype(jnp.bfloat16)
    grad_out = lax.dot_general(hidden, d_out, (((0,), (0,)), ((), ())), preferred_element_type=jnp.float32)
    d_hidden = lax.dot_general(d_out, cast_out, (((1,), (1,)), ((), ())), preferred_element_type=jnp.float32)
    d_preact = (d_hidden * (normal_cdf(preact) + preact * normal_pdf(preact))).astype(jnp.bfloat16)
    grad_in = lax.dot_general(batch_x, d_preact, (((0,), (0,)), ((), ())), preferred_element_type=jnp.float32)
    moment_in = (MOMENTUM * moment_in.astype(jnp.float32) + grad_in).astype(jnp.bfloat16)
    moment_out = (MOMENTUM * moment_out.astype(jnp.float32) + grad_out).astype(jnp.bfloat16)
    weight_in = weight_in - LEARN_RATE * moment_in.astype(jnp.float32)
    weight_out = weight_out - LEARN_RATE * moment_out.astype(jnp.float32)
    return (weight_in, weight_out, moment_in, moment_out)


def invert(order):
    count = order.shape[0]
    places = jnp.arange(count, dtype=jnp.int32)
    matches = order[:, None] == places[None, :]
    return jnp.sum(jnp.where(matches, places[:, None], 0), axis=0).astype(jnp.int32)


def reference(features, targets, row_index, hop_order, weight_in, weight_out, moment_in, moment_out):
    shard_x = features.reshape(MODELS, SHARD_ROWS, D)
    shard_y = targets.reshape(MODELS, SHARD_ROWS, D)
    model = (weight_in, weight_out, moment_in, moment_out)
    for visit_index in range(VISITS):
        def one_visit(model_one, feats_one, goals_one, index_one):
            for step_index in range(STEPS):
                picks = index_one[visit_index, step_index]
                model_one = train_step(model_one, jnp.take(feats_one, picks, axis=0), jnp.take(goals_one, picks, axis=0))
            return model_one
        model = jax.vmap(one_visit)(model, shard_x, shard_y, row_index)
        source = invert(hop_order[visit_index])
        model = tuple(jnp.take(member, source, axis=0) for member in model)
    return model
```

```python
import functools

import jax
import jax.numpy as jnp
from jax import lax
from jax.experimental import pallas as pl
from jax.experimental.pallas import tpu as pltpu
from jax.sharding import PartitionSpec as P

MOMENTUM = 0.9
LEARN_RATE = 0.1
SUB, LANE = 8, 128
F32, BF16 = jnp.float32, jnp.bfloat16
HALF_ROOT = 0.7071067811865476
PDF_SCALE = 0.3989422804014327


def tiles_of(shape):
    rows, cols = shape[-2:]
    return [
        (row * SUB, col * LANE) for row in range(rows // SUB) for col in range(cols // LANE)
    ]


def tile_slots(shapes, devices):
    slots, base = [], 0
    for shape in shapes:
        tiles = tiles_of(shape)
        if len(tiles) % devices:
            raise ValueError("uneven tiles")
        each = len(tiles) // devices
        slots.append(
            [(index // each, base + index % each, *tile) for index, tile in enumerate(tiles)]
        )
        base += each
    return slots, base


def pack(refs, slots, packed_ref):
    for ref, places in zip(refs, slots):
        for chunk, slot, row, col in places:
            packed_ref[chunk, slot] = ref[row : row + SUB, col : col + LANE].astype(
                packed_ref.dtype
            )


def unpack(packed_ref, slots, refs):
    for ref, places in zip(refs, slots):
        for chunk, slot, row, col in places:
            ref[row : row + SUB, col : col + LANE] = packed_ref[chunk, slot].astype(ref.dtype)


def train_step(x_ref, y_ref, win, wout, min_, mout, hid, dout, dpre, block):
    rows = x_ref.shape[0]
    cast_in = win[...].astype(BF16)
    cast_out = wout[...].astype(BF16)
    for start in range(0, rows, block):
        part = slice(start, start + block)
        batch_x = x_ref[part, :]
        preact = jnp.dot(batch_x, cast_in, preferred_element_type=F32)
        cdf = 0.5 * (1.0 + lax.erf(preact * HALF_ROOT))
        pdf = PDF_SCALE * jnp.exp(-0.5 * preact * preact)
        hidden = (preact * cdf).astype(BF16)
        hid[part, :] = hidden
        error = (
            batch_x.astype(F32)
            + jnp.dot(hidden, cast_out, preferred_element_type=F32)
            - y_ref[part, :].astype(F32)
        )
        d_out = (error * (1.0 / rows)).astype(BF16)
        dout[part, :] = d_out
        d_hidden = lax.dot_general(
            d_out, cast_out, (((1,), (1,)), ((), ())), preferred_element_type=F32
        )
        dpre[part, :] = (d_hidden * (cdf + preact * pdf)).astype(BF16)
    over_rows = (((0,), (0,)), ((), ()))
    grad = lax.dot_general(hid[...], dout[...], over_rows, preferred_element_type=F32)
    moment = (MOMENTUM * mout[...].astype(F32) + grad).astype(BF16)
    mout[...] = moment
    wout[...] = wout[...] - LEARN_RATE * moment.astype(F32)
    grad = lax.dot_general(x_ref[...], dpre[...], over_rows, preferred_element_type=F32)
    moment = (MOMENTUM * min_[...].astype(F32) + grad).astype(BF16)
    min_[...] = moment
    win[...] = win[...] - LEARN_RATE * moment.astype(F32)


def visit_kernel(slots, packed_input, block, *refs):
    if packed_input:
        x_ref, y_ref, arrived, sent, *scratch = refs
    else:
        x_ref, y_ref, *model, sent = refs[:7]
        scratch = refs[7:]
    state, work = scratch[:4], scratch[4:]
    step = pl.program_id(0)

    @pl.when(step == 0)
    def _():
        if packed_input:
            unpack(arrived, slots, state)
        else:
            for held, given in zip(state, model):
                held[...] = given[...]

    train_step(x_ref, y_ref, *state, *work, block)

    @pl.when(step == pl.num_programs(0) - 1)
    def _():
        pack(state, slots, sent)


def whole(shape):
    return pl.BlockSpec(shape, lambda step: (0,) * len(shape))


def visit(batch_x, batch_y, model, shapes, steps, slots, packed_shape):
    rows, width = batch_x.shape[0] // steps, batch_x.shape[1]
    hidden = shapes[0][1]
    packed_input = len(model) == 1
    batch_spec = pl.BlockSpec((rows, width), lambda step: (step, 0))
    flops = steps * 10 * rows * width * hidden
    return pl.pallas_call(
        functools.partial(visit_kernel, slots, packed_input, rows // 4),
        grid=(steps,),
        in_specs=[batch_spec, batch_spec] + [whole(member.shape) for member in model],
        out_specs=whole(packed_shape),
        out_shape=jax.ShapeDtypeStruct(packed_shape, BF16),
        scratch_shapes=[
            pltpu.VMEM(shapes[0], F32),
            pltpu.VMEM(shapes[1], F32),
            pltpu.VMEM(shapes[2], BF16),
            pltpu.VMEM(shapes[3], BF16),
            pltpu.VMEM((rows, hidden), BF16),
            pltpu.VMEM((rows, width), BF16),
            pltpu.VMEM((rows, hidden), BF16),
        ],
        cost_estimate=pl.CostEstimate(
            flops=flops,
            bytes_accessed=4 * batch_x.size + 8 * width * hidden * 4,
            transcendentals=2 * steps * rows * hidden,
        ),
        name="visit",
    )(batch_x, batch_y, *model)


def reorder_kernel(source_ref, packed_ref, out_ref, sems):
    count = out_ref.shape[0]
    copies = [
        pltpu.make_async_copy(packed_ref.at[source_ref[slot]], out_ref.at[slot], sems.at[slot])
        for slot in range(count)
    ]
    for copy in copies:
        copy.start()
    for copy in copies:
        copy.wait()


def reorder(packed, source):
    return pl.pallas_call(
        reorder_kernel,
        in_specs=[
            pl.BlockSpec(memory_space=pltpu.SMEM),
            pl.BlockSpec(memory_space=pl.ANY),
        ],
        out_specs=pl.BlockSpec(memory_space=pltpu.VMEM),
        out_shape=jax.ShapeDtypeStruct(packed.shape, packed.dtype),
        scratch_shapes=[pltpu.SemaphoreType.DMA((packed.shape[0],))],
        name="reorder",
    )(source, packed)


def unpack_kernel(slots, packed_ref, *out_refs):
    unpack(packed_ref, slots, out_refs)


def invert(order):
    count = order.shape[0]
    places = jnp.arange(count, dtype=jnp.int32)
    matches = order[:, None] == places[None, :]
    return jnp.sum(jnp.where(matches, places[:, None], 0), axis=0).astype(jnp.int32)


def exchange(packed):
    return lax.all_to_all(packed, "hop", split_axis=0, concat_axis=0, tiled=True)


def move(packed, source):
    return exchange(reorder(exchange(packed), source))


def on_device(
    features, targets, row_index, hop_order, weight_in, weight_out, moment_in, moment_out
):
    devices = lax.axis_size("hop")
    model = (weight_in[0], weight_out[0], moment_in[0], moment_out[0])
    shapes = [member.shape for member in model]
    slots, depth = tile_slots(shapes, devices)
    packed_shape = (devices, depth, SUB, LANE)
    _, visits, steps, _ = row_index.shape
    sources = [invert(hop_order[visit_index]) for visit_index in range(visits)]
    held = model
    for visit_index in range(visits):
        picks = row_index[0, visit_index].reshape(-1)
        batch_x = features.at[picks].get(mode="promise_in_bounds")
        batch_y = targets.at[picks].get(mode="promise_in_bounds")
        packed = visit(batch_x, batch_y, held, shapes, steps, slots, packed_shape)
        held = (move(packed, sources[visit_index]),)
    outs = pl.pallas_call(
        functools.partial(unpack_kernel, slots),
        out_shape=[jax.ShapeDtypeStruct(m.shape, m.dtype) for m in model],
        name="unpack",
    )(held[0])
    return tuple(member[None] for member in outs)


def solution(mesh):
    split = P(("groups", "hop"), None, None)
    in_specs = (
        P(("groups", "hop"), None),
        P(("groups", "hop"), None),
        P(("groups", "hop"), None, None, None),
        P("groups", None),
        split,
        split,
        split,
        split,
    )
    return jax.shard_map(
        on_device, mesh=mesh, in_specs=in_specs, out_specs=(split,) * 4, check_vma=False
    )
```

```python
import functools

import jax
import jax.numpy as jnp
from jax import lax
from jax.experimental import pallas as pl
from jax.experimental.pallas import tpu as pltpu
from jax.sharding import PartitionSpec as P


MOMENTUM = 0.9
LEARN_RATE = 0.1
SUB, LANE = 8, 128
F32, BF16 = jnp.float32, jnp.bfloat16
HALF_ROOT = 0.7071067811865476
PDF_SCALE = 0.3989422804014327


def tile_slots(shapes, pieces):
    slots, base = [], 0
    for rows, cols in shapes:
        tiles = [(row, col) for row in range(0, rows, SUB) for col in range(0, cols, LANE)]
        if len(tiles) % pieces:
            raise ValueError("uneven tiles")
        each = len(tiles) // pieces
        slots.append(
            [(index // each, base + index % each, *tile) for index, tile in enumerate(tiles)]
        )
        base += each
    return slots, base


def pack(refs, slots, packed_ref):
    for ref, places in zip(refs, slots):
        for piece, slot, row, col in places:
            packed_ref[piece, slot] = ref[row : row + SUB, col : col + LANE].astype(
                packed_ref.dtype
            )


def unpack(packed_ref, slots, refs):
    for ref, places in zip(refs, slots):
        for piece, slot, row, col in places:
            ref[row : row + SUB, col : col + LANE] = packed_ref[piece, slot].astype(ref.dtype)


def collect(me_ref, piece_refs, packed_ref, sems):
    chip = me_ref[0] // 2
    return [
        pltpu.make_async_copy(ref, packed_ref.at[chip ^ k], sems.at[k])
        for k, ref in enumerate(piece_refs)
    ]


def scatter(me_ref, packed_ref, piece_refs, sems):
    chip = me_ref[0] // 2
    return [
        pltpu.make_async_copy(packed_ref.at[chip ^ k], ref, sems.at[k])
        for k, ref in enumerate(piece_refs)
    ]


def train_step(x_ref, y_ref, win, wout, min_, mout, hid, dout, dpre, block):
    rows = x_ref.shape[0]
    cast_in = win[...].astype(BF16)
    cast_out = wout[...].astype(BF16)
    for start in range(0, rows, block):
        part = slice(start, start + block)
        batch_x = x_ref[part, :]
        preact = jnp.dot(batch_x, cast_in, preferred_element_type=F32)
        cdf = 0.5 * (1.0 + lax.erf(preact * HALF_ROOT))
        pdf = PDF_SCALE * jnp.exp(-0.5 * preact * preact)
        hidden = (preact * cdf).astype(BF16)
        hid[part, :] = hidden
        error = (
            batch_x.astype(F32)
            + jnp.dot(hidden, cast_out, preferred_element_type=F32)
            - y_ref[part, :].astype(F32)
        )
        d_out = (error * (1.0 / rows)).astype(BF16)
        dout[part, :] = d_out
        d_hidden = lax.dot_general(
            d_out, cast_out, (((1,), (1,)), ((), ())), preferred_element_type=F32
        )
        dpre[part, :] = (d_hidden * (cdf + preact * pdf)).astype(BF16)
    over_rows = (((0,), (0,)), ((), ()))
    grad = lax.dot_general(hid[...], dout[...], over_rows, preferred_element_type=F32)
    moment = (MOMENTUM * mout[...].astype(F32) + grad).astype(BF16)
    mout[...] = moment
    wout[...] = wout[...] - LEARN_RATE * moment.astype(F32)
    grad = lax.dot_general(x_ref[...], dpre[...], over_rows, preferred_element_type=F32)
    moment = (MOMENTUM * min_[...].astype(F32) + grad).astype(BF16)
    min_[...] = moment
    win[...] = win[...] - LEARN_RATE * moment.astype(F32)


def visit_kernel(slots, pieces, packed_input, block, *refs):
    inputs = 2 * pieces if packed_input else 4
    me_ref, x_ref, y_ref = refs[:3]
    given = refs[3 : 3 + inputs]
    sent = refs[3 + inputs : 3 + inputs + 2 * pieces]
    scratch = refs[3 + inputs + 2 * pieces :]
    state, work = scratch[:4], scratch[4:7]
    packed, sems = scratch[7:9], scratch[9]
    step = pl.program_id(0)
    halves = [(slots[:2], state[:2]), (slots[2:], state[2:])]

    @pl.when(step == 0)
    def _():
        if packed_input:
            copies = [
                collect(me_ref, given[half * pieces :][:pieces], packed[half], sems.at[half])
                for half in range(2)
            ]
            for copy in copies[0] + copies[1]:
                copy.start()
            for half, (places, held) in enumerate(halves):
                for copy in copies[half]:
                    copy.wait()
                unpack(packed[half], places, held)
        else:
            for held, ref in zip(state, given):
                held[...] = ref[...]

    train_step(x_ref, y_ref, *state, *work, block)

    @pl.when(step == pl.num_programs(0) - 1)
    def _():
        copies = []
        for half, (places, held) in enumerate(halves):
            pack(held, places, packed[half])
            own = scatter(me_ref, packed[half], sent[half * pieces :][:pieces], sems.at[half])
            for copy in own:
                copy.start()
            copies += own
        for copy in copies:
            copy.wait()


def whole(shape):
    return pl.BlockSpec(shape, lambda step: (0,) * len(shape))


SCALARS = pl.BlockSpec(memory_space=pltpu.SMEM)
ANYWHERE = pl.BlockSpec(memory_space=pl.ANY)


def visit(me, batch_x, batch_y, model, shapes, steps, slots, piece_shape, pieces):
    rows, width = batch_x.shape[0] // steps, batch_x.shape[1]
    hidden = shapes[0][1]
    packed_input = len(model) > 4
    batch_spec = pl.BlockSpec((rows, width), lambda step: (step, 0))
    model_specs = [ANYWHERE if packed_input else whole(member.shape) for member in model]
    outs = pl.pallas_call(
        functools.partial(visit_kernel, slots, pieces, packed_input, rows // 4),
        grid=(steps,),
        in_specs=[SCALARS, batch_spec, batch_spec] + model_specs,
        out_specs=[ANYWHERE] * (2 * pieces),
        out_shape=[jax.ShapeDtypeStruct(piece_shape, BF16)] * (2 * pieces),
        scratch_shapes=[
            pltpu.VMEM(shapes[0], F32),
            pltpu.VMEM(shapes[1], F32),
            pltpu.VMEM(shapes[2], BF16),
            pltpu.VMEM(shapes[3], BF16),
            pltpu.VMEM((rows, hidden), BF16),
            pltpu.VMEM((rows, width), BF16),
            pltpu.VMEM((rows, hidden), BF16),
            pltpu.VMEM((pieces, *piece_shape), BF16),
            pltpu.VMEM((pieces, *piece_shape), BF16),
            pltpu.SemaphoreType.DMA((2, pieces)),
        ],
        cost_estimate=pl.CostEstimate(
            flops=steps * 10 * rows * width * hidden,
            bytes_accessed=4 * batch_x.size + 8 * width * hidden * 4,
            transcendentals=2 * steps * rows * hidden,
        ),
        name="visit",
    )(me, batch_x, batch_y, *model)
    return outs[:pieces], outs[pieces:]


def route_kernel(pieces, me_ref, source_ref, own_ref, partner_ref, *refs):
    out_refs, sems = refs[:pieces], refs[pieces]
    chip, core = me_ref[0] // 2, me_ref[0] % 2
    for k, out_ref in enumerate(out_refs):
        source = source_ref[2 * (chip ^ k) + core]
        place = chip ^ (source // 2)

        @pl.when(source % 2 == core)
        def _():
            pltpu.make_async_copy(own_ref.at[place], out_ref, sems.at[k]).start()

        @pl.when(source % 2 != core)
        def _():
            pltpu.make_async_copy(partner_ref.at[place], out_ref, sems.at[k]).start()

    for k, out_ref in enumerate(out_refs):
        pltpu.make_async_copy(own_ref.at[0], out_ref, sems.at[k]).wait()


def route(me, source, own, partner):
    pieces = own.shape[0]
    in_vmem = pl.BlockSpec(memory_space=pltpu.VMEM)
    return pl.pallas_call(
        functools.partial(route_kernel, pieces),
        in_specs=[SCALARS, SCALARS, in_vmem, in_vmem],
        out_specs=[ANYWHERE] * pieces,
        out_shape=[jax.ShapeDtypeStruct(own.shape[1:], own.dtype)] * pieces,
        scratch_shapes=[pltpu.SemaphoreType.DMA((pieces,))],
        cost_estimate=pl.CostEstimate(
            flops=0, bytes_accessed=4 * own.size, transcendentals=0
        ),
        name="route",
    )(me, source, own, partner)


def unpack_kernel(slots, pieces, me_ref, *refs):
    given, outs, (packed, sems) = refs[:pieces], refs[pieces:-2], refs[-2:]
    copies = collect(me_ref, given, packed, sems)
    for copy in copies:
        copy.start()
    for copy in copies:
        copy.wait()
    unpack(packed, slots, outs)


def unpacked(me, given, slots, outs):
    pieces = len(given)
    return pl.pallas_call(
        functools.partial(unpack_kernel, slots, pieces),
        in_specs=[SCALARS] + [ANYWHERE] * pieces,
        out_shape=[jax.ShapeDtypeStruct(shape, dtype) for shape, dtype in outs],
        scratch_shapes=[
            pltpu.VMEM((pieces, *given[0].shape), BF16),
            pltpu.SemaphoreType.DMA((pieces,)),
        ],
        name="unpack",
    )(me, *given)


def invert(order):
    count = order.shape[0]
    places = jnp.arange(count, dtype=jnp.int32)
    matches = order[:, None] == places[None, :]
    return jnp.sum(jnp.where(matches, places[:, None], 0), axis=0).astype(jnp.int32)


def spread(parts, devices):
    moved = [None] * len(parts)
    moved[0] = parts[0]
    for k in sorted(range(1, len(parts)), reverse=True):
        moved[k] = lax.ppermute(parts[k], "hop", [(i, i ^ (2 * k)) for i in range(devices)])
    return moved


def move(parts, me, source, devices):
    own = spread(parts, devices)
    own = jnp.stack(own)
    partner = lax.ppermute(own, "hop", [(i, i ^ 1) for i in range(devices)])
    routed = route(me, source, own, partner)
    return spread(routed, devices)


def on_device(
    features, targets, row_index, hop_order, weight_in, weight_out, moment_in, moment_out
):
    devices = lax.axis_size("hop")
    me = lax.axis_index("hop").astype(jnp.int32).reshape(1)
    model = (weight_in[0], weight_out[0], moment_in[0], moment_out[0])
    shapes = [member.shape for member in model]
    pieces = devices // 2
    slots, depth = tile_slots(shapes[:2], pieces)
    piece_shape = (depth, SUB, LANE)
    _, visits, steps, _ = row_index.shape
    sources = [invert(hop_order[visit_index]) for visit_index in range(visits)]
    held = model
    for visit_index in range(visits):
        picks = row_index[0, visit_index].reshape(-1)
        batch_x = features.at[picks].get(mode="promise_in_bounds")
        batch_y = targets.at[picks].get(mode="promise_in_bounds")
        weights, moments = visit(
            me, batch_x, batch_y, held, shapes, steps, slots * 2, piece_shape, pieces
        )
        source = sources[visit_index]
        weights = move(weights, me, source, devices)
        moments = move(moments, me, source, devices)
        held = (*weights, *moments)
    outs = unpacked(me, weights, slots, [(m.shape, m.dtype) for m in model[:2]])
    outs += unpacked(me, moments, slots, [(m.shape, m.dtype) for m in model[2:]])
    return tuple(member[None] for member in outs)


def solution(mesh):
    split = P(("groups", "hop"), None, None)
    in_specs = (
        P(("groups", "hop"), None),
        P(("groups", "hop"), None),
        P(("groups", "hop"), None, None, None),
        P("groups", None),
        split,
        split,
        split,
        split,
    )
    return jax.shard_map(
        on_device, mesh=mesh, in_specs=in_specs, out_specs=(split,) * 4, check_vma=False
    )
```

```python
import functools

import jax
import jax.numpy as jnp
from jax import lax
from jax.experimental import pallas as pl
from jax.experimental.pallas import tpu as pltpu
from jax.sharding import PartitionSpec as P

MOMENTUM = 0.9
LEARN_RATE = 0.1
SUB, LANE = 8, 128
MIB = 1 << 20
FETCH_BLOCKS, UNROLL, UNPACK_BLOCKS = 4, 16, 4
F32, BF16 = jnp.float32, jnp.bfloat16
HALF_ROOT = 0.7071067811865476
PDF_SCALE = 0.3989422804014327


def fetch_kernel(visit_index, picks_ref, x_ref, y_ref, x_out, y_out, held, table, picked, sems):
    count, width = x_ref.shape
    block, lanes = count // FETCH_BLOCKS, width // LANE
    copies = []
    for part in range(FETCH_BLOCKS):
        place = pl.ds(part * block, block)
        for side, ref in enumerate((x_ref, y_ref)):
            copies.append(
                pltpu.make_async_copy(
                    ref.at[place], held.at[side, place], sems.at[FETCH_BLOCKS * side + part]
                )
            )
            copies[-1].start()
    for part in range(FETCH_BLOCKS):
        for side in range(2):
            copies[2 * part + side].wait()
            for lane in range(lanes):
                place = pl.ds(part * block * SUB + side * lanes + lane, block, stride=SUB)
                table[place, :] = held[
                    side, part * block : (part + 1) * block, lane * LANE : (lane + 1) * LANE
                ].astype(F32)
    _, _, steps, rows = picks_ref.shape
    for step in range(steps):

        @pl.loop(0, rows // UNROLL)
        def _(group):
            for offset in range(UNROLL):
                row = group * UNROLL + offset
                pick = picks_ref[0, visit_index, step, row]
                source = pl.multiple_of(pick * SUB, SUB)
                target = pl.multiple_of((step * rows + row) * SUB, SUB)
                picked[pl.ds(target, SUB), :] = table[pl.ds(source, SUB), :]

    for side, ref in enumerate((x_out, y_out)):
        for lane in range(lanes):
            place = pl.ds(side * lanes + lane, steps * rows, stride=SUB)
            ref[:, lane * LANE : (lane + 1) * LANE] = picked[place, :].astype(ref.dtype)


def fetch(features, targets, row_index, visit_index):
    count, width = features.shape
    _, _, steps, rows = row_index.shape
    if 2 * width > SUB * LANE or count % FETCH_BLOCKS or rows % UNROLL:
        raise ValueError("sizes")
    total = steps * rows
    return pl.pallas_call(
        functools.partial(fetch_kernel, visit_index),
        in_specs=[
            pl.BlockSpec(memory_space=pltpu.SMEM),
            pl.BlockSpec(memory_space=pl.ANY),
            pl.BlockSpec(memory_space=pl.ANY),
        ],
        out_specs=[pl.BlockSpec(memory_space=pltpu.VMEM)] * 2,
        out_shape=[jax.ShapeDtypeStruct((total, width), features.dtype)] * 2,
        scratch_shapes=[
            pltpu.VMEM((2, count, width), features.dtype),
            pltpu.VMEM((count * SUB, LANE), F32),
            pltpu.VMEM((total * SUB, LANE), F32),
            pltpu.SemaphoreType.DMA((2 * FETCH_BLOCKS,)),
        ],
        compiler_params=pltpu.CompilerParams(vmem_limit_bytes=57 * MIB),
        cost_estimate=pl.CostEstimate(
            flops=0, bytes_accessed=4 * count * width, transcendentals=0
        ),
        name="fetch",
    )(row_index, features, targets)


def tiles_of(shape):
    rows, cols = shape[-2:]
    return [
        (row * SUB, col * LANE) for row in range(rows // SUB) for col in range(cols // LANE)
    ]


def tile_slots(shapes, devices):
    slots, base = [], 0
    for shape in shapes:
        tiles = tiles_of(shape)
        if len(tiles) % devices:
            raise ValueError("uneven tiles")
        each = len(tiles) // devices
        slots.append(
            [(index // each, base + index % each, *tile) for index, tile in enumerate(tiles)]
        )
        base += each
    return slots, base


def pack(refs, slots, packed_ref):
    for ref, places in zip(refs, slots):
        for chunk, slot, row, col in places:
            packed_ref[chunk, slot] = ref[row : row + SUB, col : col + LANE].astype(
                packed_ref.dtype
            )


def unpack(packed_ref, slots, refs):
    for ref, places in zip(refs, slots):
        for chunk, slot, row, col in places:
            ref[row : row + SUB, col : col + LANE] = packed_ref[chunk, slot].astype(ref.dtype)


def train_step(x_ref, y_ref, win, wout, min_, mout, hid, dout, dpre, block):
    rows = x_ref.shape[0]
    cast_in = win[...].astype(BF16)
    cast_out = wout[...].astype(BF16)
    for start in range(0, rows, block):
        part = slice(start, start + block)
        batch_x = x_ref[part, :]
        preact = jnp.dot(batch_x, cast_in, preferred_element_type=F32)
        cdf = 0.5 * (1.0 + lax.erf(preact * HALF_ROOT))
        pdf = PDF_SCALE * jnp.exp(-0.5 * preact * preact)
        hidden = (preact * cdf).astype(BF16)
        hid[part, :] = hidden
        error = (
            batch_x.astype(F32)
            + jnp.dot(hidden, cast_out, preferred_element_type=F32)
            - y_ref[part, :].astype(F32)
        )
        d_out = (error * (1.0 / rows)).astype(BF16)
        dout[part, :] = d_out
        d_hidden = lax.dot_general(
            d_out, cast_out, (((1,), (1,)), ((), ())), preferred_element_type=F32
        )
        dpre[part, :] = (d_hidden * (cdf + preact * pdf)).astype(BF16)
    over_rows = (((0,), (0,)), ((), ()))
    grad = lax.dot_general(hid[...], dout[...], over_rows, preferred_element_type=F32)
    moment = (MOMENTUM * mout[...].astype(F32) + grad).astype(BF16)
    mout[...] = moment
    wout[...] = wout[...] - LEARN_RATE * moment.astype(F32)
    grad = lax.dot_general(x_ref[...], dpre[...], over_rows, preferred_element_type=F32)
    moment = (MOMENTUM * min_[...].astype(F32) + grad).astype(BF16)
    min_[...] = moment
    win[...] = win[...] - LEARN_RATE * moment.astype(F32)


def visit_kernel(slots, packed_input, block, *refs):
    if packed_input:
        x_ref, y_ref, arrived, sent, *scratch = refs
    else:
        x_ref, y_ref, *model, sent = refs[:7]
        scratch = refs[7:]
    state, work = scratch[:4], scratch[4:]
    step = pl.program_id(0)

    @pl.when(step == 0)
    def _():
        if packed_input:
            unpack(arrived, slots, state)
        else:
            for held, given in zip(state, model):
                held[...] = given[...]

    train_step(x_ref, y_ref, *state, *work, block)

    @pl.when(step == pl.num_programs(0) - 1)
    def _():
        pack(state, slots, sent)


def whole(shape):
    return pl.BlockSpec(shape, lambda step: (0,) * len(shape))


def visit(batch_x, batch_y, model, shapes, steps, slots, packed_shape):
    rows, width = batch_x.shape[0] // steps, batch_x.shape[1]
    hidden = shapes[0][1]
    packed_input = len(model) == 1
    batch_spec = pl.BlockSpec((rows, width), lambda step: (step, 0))
    flops = steps * 10 * rows * width * hidden
    return pl.pallas_call(
        functools.partial(visit_kernel, slots, packed_input, rows // 4),
        grid=(steps,),
        in_specs=[batch_spec, batch_spec] + [whole(member.shape) for member in model],
        out_specs=whole(packed_shape),
        out_shape=jax.ShapeDtypeStruct(packed_shape, BF16),
        scratch_shapes=[
            pltpu.VMEM(shapes[0], F32),
            pltpu.VMEM(shapes[1], F32),
            pltpu.VMEM(shapes[2], BF16),
            pltpu.VMEM(shapes[3], BF16),
            pltpu.VMEM((rows, hidden), BF16),
            pltpu.VMEM((rows, width), BF16),
            pltpu.VMEM((rows, hidden), BF16),
        ],
        cost_estimate=pl.CostEstimate(
            flops=flops,
            bytes_accessed=4 * batch_x.size + 8 * width * hidden * 4,
            transcendentals=2 * steps * rows * hidden,
        ),
        compiler_params=pltpu.CompilerParams(vmem_limit_bytes=28 * MIB),
        name="visit",
    )(batch_x, batch_y, *model)


def reorder_kernel(source_ref, packed_ref, out_ref, sems):
    copies = [
        pltpu.make_async_copy(packed_ref.at[source_ref[slot]], out_ref.at[slot], sems.at[slot])
        for slot in range(out_ref.shape[0])
    ]
    for copy in copies:
        copy.start()
    for copy in copies:
        copy.wait()


def reorder(packed, source):
    return pl.pallas_call(
        reorder_kernel,
        in_specs=[
            pl.BlockSpec(memory_space=pltpu.SMEM),
            pl.BlockSpec(memory_space=pltpu.VMEM),
        ],
        out_specs=pl.BlockSpec(memory_space=pl.ANY),
        out_shape=jax.ShapeDtypeStruct(packed.shape, packed.dtype),
        scratch_shapes=[pltpu.SemaphoreType.DMA((packed.shape[0],))],
        compiler_params=pltpu.CompilerParams(vmem_limit_bytes=8 * MIB),
        name="reorder",
    )(source, packed)


def unpack_blocks(packed, outs, devices):
    blocks = UNPACK_BLOCKS if devices % UNPACK_BLOCKS == 0 else 1
    parts = [(shape[0] // blocks, shape[1]) for shape, _ in outs]
    slots, _ = tile_slots(parts, devices // blocks)
    return pl.pallas_call(
        functools.partial(unpack_kernel, slots),
        grid=(blocks,),
        in_specs=[
            pl.BlockSpec((devices // blocks, *packed.shape[1:]), lambda block: (block, 0, 0, 0))
        ],
        out_specs=[pl.BlockSpec(part, lambda block: (block, 0)) for part in parts],
        out_shape=[jax.ShapeDtypeStruct(shape, dtype) for shape, dtype in outs],
        compiler_params=pltpu.CompilerParams(vmem_limit_bytes=16 * MIB),
        name="unpack",
    )(packed)


def unpack_kernel(slots, packed_ref, *out_refs):
    unpack(packed_ref, slots, out_refs)


def invert(order):
    count = order.shape[0]
    places = jnp.arange(count, dtype=jnp.int32)
    matches = order[:, None] == places[None, :]
    return jnp.sum(jnp.where(matches, places[:, None], 0), axis=0).astype(jnp.int32)


def exchange(packed):
    return lax.all_to_all(packed, "hop", split_axis=0, concat_axis=0, tiled=True)


def move(packed, source):
    return exchange(reorder(exchange(packed), source))


def on_device(
    features, targets, row_index, hop_order, weight_in, weight_out, moment_in, moment_out
):
    devices = lax.axis_size("hop")
    model = (weight_in[0], weight_out[0], moment_in[0], moment_out[0])
    shapes = [member.shape for member in model]
    slots, depth = tile_slots(shapes, devices)
    packed_shape = (devices, depth, SUB, LANE)
    _, visits, steps, _ = row_index.shape
    sources = [invert(hop_order[visit_index]) for visit_index in range(visits)]
    held = model
    for visit_index in range(visits):
        batch_x, batch_y = fetch(features, targets, row_index, visit_index)
        packed = visit(batch_x, batch_y, held, shapes, steps, slots, packed_shape)
        held = (move(packed, sources[visit_index]),)
    outs = unpack_blocks(held[0], [(m.shape, m.dtype) for m in model], devices)
    return tuple(member[None] for member in outs)


def solution(mesh):
    split = P(("groups", "hop"), None, None)
    in_specs = (
        P(("groups", "hop"), None),
        P(("groups", "hop"), None),
        P(("groups", "hop"), None, None, None),
        P("groups", None),
        split,
        split,
        split,
        split,
    )
    return jax.shard_map(
        on_device, mesh=mesh, in_specs=in_specs, out_specs=(split,) * 4, check_vma=False
    )
```

```python
import functools

import jax
import jax.numpy as jnp
from jax import lax
from jax.experimental import pallas as pl
from jax.experimental.pallas import tpu as pltpu
from jax.sharding import PartitionSpec as P

MOMENTUM = 0.9
LEARN_RATE = 0.1
SUB, LANE = 8, 128
MIB = 1 << 20
STRIDE = SUB + 1
FETCH_BLOCKS, UNROLL, UNPACK_BLOCKS = 4, 16, 4
FIRST_MIB, FETCH_MIB, LATER_MIB = 58, 58, 28
F32, BF16 = jnp.float32, jnp.bfloat16
HALF_ROOT = 0.7071067811865476
PDF_SCALE = 0.3989422804014327


def table_copies(x_ref, y_ref, held, sems):
    count = x_ref.shape[0]
    block = count // FETCH_BLOCKS
    copies = []
    for part in range(FETCH_BLOCKS):
        place = pl.ds(part * block, block)
        for side, ref in enumerate((x_ref, y_ref)):
            copies.append(
                pltpu.make_async_copy(ref.at[place], held.at[side, place], sems.at[2 * part + side])
            )
    return copies


def build_table(copies, held, table):
    _, count, width = held.shape
    block, lanes = count // FETCH_BLOCKS, width // LANE
    for part in range(FETCH_BLOCKS):
        for side in range(2):
            copies[2 * part + side].wait()
            for lane in range(lanes):
                place = pl.ds(part * block * STRIDE + side * lanes + lane, block, stride=STRIDE)
                table[place, :] = held[
                    side, part * block : (part + 1) * block, lane * LANE : (lane + 1) * LANE
                ].astype(F32)


def pick_rows(picks_ref, step, visit_index, table, picked, outs, first):
    rows = picks_ref.shape[3]

    @pl.loop(0, rows // UNROLL)
    def _(group):
        for offset in range(UNROLL):
            row = group * UNROLL + offset
            pick = picks_ref[0, step, visit_index, row]
            picked[pl.ds(row * STRIDE, SUB), :] = table[pl.ds(pick * STRIDE, SUB), :]

    lanes = outs[0].shape[1] // LANE
    for side, ref in enumerate(outs):
        for lane in range(lanes):
            place = pl.ds(side * lanes + lane, rows, stride=STRIDE)
            ref[first : first + rows, lane * LANE : (lane + 1) * LANE] = picked[place, :].astype(
                ref.dtype
            )


def table_scratch(features, rows):
    count, width = features.shape
    if 2 * width > SUB * LANE or count % FETCH_BLOCKS or rows % UNROLL:
        raise ValueError("sizes")
    return [
        pltpu.VMEM((2, count, width), features.dtype),
        pltpu.VMEM((count * STRIDE, LANE), F32),
        pltpu.VMEM((rows * STRIDE, LANE), F32),
        pltpu.SemaphoreType.DMA((2 * FETCH_BLOCKS,)),
    ]


def fetch_kernel(visit_index, picks_ref, x_ref, y_ref, x_out, y_out, held, table, picked, sems):
    _, steps, _, rows = picks_ref.shape
    copies = table_copies(x_ref, y_ref, held, sems)
    for copy in copies:
        copy.start()
    build_table(copies, held, table)
    for step in range(steps):
        pick_rows(picks_ref, step, visit_index, table, picked, (x_out, y_out), step * rows)


def fetch(features, targets, picks, visit_index):
    count, width = features.shape
    _, steps, _, rows = picks.shape
    return pl.pallas_call(
        functools.partial(fetch_kernel, visit_index),
        in_specs=[SCALARS, ANYWHERE, ANYWHERE],
        out_specs=[pl.BlockSpec(memory_space=pltpu.VMEM)] * 2,
        out_shape=[jax.ShapeDtypeStruct((steps * rows, width), features.dtype)] * 2,
        scratch_shapes=table_scratch(features, rows),
        compiler_params=pltpu.CompilerParams(vmem_limit_bytes=FETCH_MIB * MIB),
        cost_estimate=pl.CostEstimate(
            flops=0, bytes_accessed=4 * count * width, transcendentals=0
        ),
        name="fetch",
    )(picks, features, targets)


def tiles_of(shape):
    rows, cols = shape[-2:]
    return [
        (row * SUB, col * LANE) for row in range(rows // SUB) for col in range(cols // LANE)
    ]


def tile_slots(shapes, devices):
    slots, base = [], 0
    for shape in shapes:
        tiles = tiles_of(shape)
        if len(tiles) % devices:
            raise ValueError("uneven tiles")
        each = len(tiles) // devices
        slots.append(
            [(index // each, base + index % each, *tile) for index, tile in enumerate(tiles)]
        )
        base += each
    return slots, base


def pack(refs, slots, packed_ref):
    for ref, places in zip(refs, slots):
        for chunk, slot, row, col in places:
            packed_ref[chunk, slot] = ref[row : row + SUB, col : col + LANE].astype(
                packed_ref.dtype
            )


def unpack(packed_ref, slots, refs):
    for ref, places in zip(refs, slots):
        for chunk, slot, row, col in places:
            ref[row : row + SUB, col : col + LANE] = packed_ref[chunk, slot].astype(ref.dtype)


def train_step(x_ref, y_ref, win, wout, min_, mout, hid, dout, dpre, block):
    rows = x_ref.shape[0]
    cast_in = win[...].astype(BF16)
    cast_out = wout[...].astype(BF16)
    for start in range(0, rows, block):
        part = slice(start, start + block)
        batch_x = x_ref[part, :]
        preact = jnp.dot(batch_x, cast_in, preferred_element_type=F32)
        cdf = 0.5 * (1.0 + lax.erf(preact * HALF_ROOT))
        pdf = PDF_SCALE * jnp.exp(-0.5 * preact * preact)
        hidden = (preact * cdf).astype(BF16)
        hid[part, :] = hidden
        error = (
            batch_x.astype(F32)
            + jnp.dot(hidden, cast_out, preferred_element_type=F32)
            - y_ref[part, :].astype(F32)
        )
        d_out = (error * (1.0 / rows)).astype(BF16)
        dout[part, :] = d_out
        d_hidden = lax.dot_general(
            d_out, cast_out, (((1,), (1,)), ((), ())), preferred_element_type=F32
        )
        dpre[part, :] = (d_hidden * (cdf + preact * pdf)).astype(BF16)
    over_rows = (((0,), (0,)), ((), ()))
    grad = lax.dot_general(hid[...], dout[...], over_rows, preferred_element_type=F32)
    moment = (MOMENTUM * mout[...].astype(F32) + grad).astype(BF16)
    mout[...] = moment
    wout[...] = wout[...] - LEARN_RATE * moment.astype(F32)
    grad = lax.dot_general(x_ref[...], dpre[...], over_rows, preferred_element_type=F32)
    moment = (MOMENTUM * min_[...].astype(F32) + grad).astype(BF16)
    min_[...] = moment
    win[...] = win[...] - LEARN_RATE * moment.astype(F32)


def later_visit_kernel(slots, block, x_ref, y_ref, arrived, sent, *scratch):
    state, work = scratch[:4], scratch[4:]
    step = pl.program_id(0)

    @pl.when(step == 0)
    def _():
        unpack(arrived, slots, state)

    train_step(x_ref, y_ref, *state, *work, block)

    @pl.when(step == pl.num_programs(0) - 1)
    def _():
        pack(state, slots, sent)


def first_visit_kernel(slots, block, picks_ref, x_ref, y_ref, *refs):
    model, sent, scratch = refs[:4], refs[4], refs[5:]
    state, work, batch = scratch[:4], scratch[4:7], scratch[7:9]
    held, table, picked, sems, model_sems = scratch[9:]
    step = pl.program_id(0)

    @pl.when(step == 0)
    def _():
        copies = table_copies(x_ref, y_ref, held, sems)
        loads = [
            pltpu.make_async_copy(ref, kept, model_sems.at[index])
            for index, (ref, kept) in enumerate(zip(model, state))
        ]
        for copy in copies + loads:
            copy.start()
        build_table(copies, held, table)
        for copy in loads:
            copy.wait()

    pick_rows(picks_ref, step, 0, table, picked, batch, 0)
    train_step(*batch, *state, *work, block)

    @pl.when(step == pl.num_programs(0) - 1)
    def _():
        pack(state, slots, sent)


def whole(shape):
    return pl.BlockSpec(shape, lambda step: (0,) * len(shape))


SCALARS = pl.BlockSpec(memory_space=pltpu.SMEM)
ANYWHERE = pl.BlockSpec(memory_space=pl.ANY)


def visit(kernel, args, in_specs, more_scratch, limit, sizes, slots, packed_shape):
    steps, rows, width, hidden = sizes
    return pl.pallas_call(
        functools.partial(kernel, slots, rows // 4),
        grid=(steps,),
        in_specs=in_specs,
        out_specs=whole(packed_shape),
        out_shape=jax.ShapeDtypeStruct(packed_shape, BF16),
        scratch_shapes=[
            pltpu.VMEM((width, hidden), F32),
            pltpu.VMEM((hidden, width), F32),
            pltpu.VMEM((width, hidden), BF16),
            pltpu.VMEM((hidden, width), BF16),
            pltpu.VMEM((rows, hidden), BF16),
            pltpu.VMEM((rows, width), BF16),
            pltpu.VMEM((rows, hidden), BF16),
            *more_scratch,
        ],
        cost_estimate=pl.CostEstimate(
            flops=steps * 10 * rows * width * hidden,
            bytes_accessed=4 * steps * rows * width + 32 * width * hidden,
            transcendentals=2 * steps * rows * hidden,
        ),
        compiler_params=pltpu.CompilerParams(vmem_limit_bytes=limit * MIB),
        name="visit",
    )(*args)


def first_visit(features, targets, picks, model, sizes, slots, packed_shape):
    _, rows, width, _ = sizes
    scratch = [pltpu.VMEM((rows, width), BF16)] * 2 + table_scratch(features, rows)
    return visit(
        first_visit_kernel,
        (picks, features, targets, *model),
        [SCALARS] + [ANYWHERE] * 6,
        scratch + [pltpu.SemaphoreType.DMA((4,))],
        FIRST_MIB,
        sizes,
        slots,
        packed_shape,
    )


def later_visit(batch, packed, sizes, slots):
    _, rows, width, _ = sizes
    batch_spec = pl.BlockSpec((rows, width), lambda step: (step, 0))
    return visit(
        later_visit_kernel,
        (*batch, packed),
        [batch_spec, batch_spec, whole(packed.shape)],
        [],
        LATER_MIB,
        sizes,
        slots,
        packed.shape,
    )


def reorder_kernel(source_ref, packed_ref, out_ref, sems):
    copies = [
        pltpu.make_async_copy(packed_ref.at[source_ref[slot]], out_ref.at[slot], sems.at[slot])
        for slot in range(out_ref.shape[0])
    ]
    for copy in copies:
        copy.start()
    for copy in copies:
        copy.wait()


def reorder(packed, source):
    return pl.pallas_call(
        reorder_kernel,
        in_specs=[
            pl.BlockSpec(memory_space=pltpu.SMEM),
            pl.BlockSpec(memory_space=pltpu.VMEM),
        ],
        out_specs=pl.BlockSpec(memory_space=pl.ANY),
        out_shape=jax.ShapeDtypeStruct(packed.shape, packed.dtype),
        scratch_shapes=[pltpu.SemaphoreType.DMA((packed.shape[0],))],
        compiler_params=pltpu.CompilerParams(vmem_limit_bytes=8 * MIB),
        name="reorder",
    )(source, packed)


def unpack_blocks(packed, outs, devices):
    blocks = UNPACK_BLOCKS if devices % UNPACK_BLOCKS == 0 else 1
    parts = [(shape[0] // blocks, shape[1]) for shape, _ in outs]
    slots, _ = tile_slots(parts, devices // blocks)
    return pl.pallas_call(
        functools.partial(unpack_kernel, slots),
        grid=(blocks,),
        in_specs=[
            pl.BlockSpec((devices // blocks, *packed.shape[1:]), lambda block: (block, 0, 0, 0))
        ],
        out_specs=[pl.BlockSpec(part, lambda block: (block, 0)) for part in parts],
        out_shape=[jax.ShapeDtypeStruct(shape, dtype) for shape, dtype in outs],
        compiler_params=pltpu.CompilerParams(vmem_limit_bytes=16 * MIB),
        name="unpack",
    )(packed)


def unpack_kernel(slots, packed_ref, *out_refs):
    unpack(packed_ref, slots, out_refs)


def invert(order):
    count = order.shape[0]
    places = jnp.arange(count, dtype=jnp.int32)
    matches = order[:, None] == places[None, :]
    return jnp.sum(jnp.where(matches, places[:, None], 0), axis=0).astype(jnp.int32)


def exchange(packed):
    return lax.all_to_all(packed, "hop", split_axis=0, concat_axis=0, tiled=True)


def move(packed, source, beside=()):
    spread = exchange(packed)
    if beside:
        spread, *beside = lax.optimization_barrier((spread, *beside))
    return exchange(reorder(spread, source)), beside


def on_device(
    features, targets, row_index, hop_order, weight_in, weight_out, moment_in, moment_out
):
    devices = lax.axis_size("hop")
    model = (weight_in[0], weight_out[0], moment_in[0], moment_out[0])
    shapes = [member.shape for member in model]
    slots, depth = tile_slots(shapes, devices)
    packed_shape = (devices, depth, SUB, LANE)
    _, visits, steps, rows = row_index.shape
    sizes = (steps, rows, *shapes[0])
    picks = jnp.transpose(row_index, (0, 2, 1, 3))
    sources = [invert(hop_order[visit_index]) for visit_index in range(visits)]
    packed = first_visit(features, targets, picks, model, sizes, slots, packed_shape)
    for visit_index in range(1, visits):
        batch = fetch(features, targets, picks, visit_index)
        packed, batch = move(packed, sources[visit_index - 1], batch)
        packed = later_visit(batch, packed, sizes, slots)
    packed, _ = move(packed, sources[-1])
    outs = unpack_blocks(packed, [(m.shape, m.dtype) for m in model], devices)
    return tuple(member[None] for member in outs)


def solution(mesh):
    split = P(("groups", "hop"), None, None)
    in_specs = (
        P(("groups", "hop"), None),
        P(("groups", "hop"), None),
        P(("groups", "hop"), None, None, None),
        P("groups", None),
        split,
        split,
        split,
        split,
    )
    return jax.shard_map(
        on_device, mesh=mesh, in_specs=in_specs, out_specs=(split,) * 4, check_vma=False
    )
```

```python
import functools

import jax
import jax.numpy as jnp
from jax import lax
from jax.experimental import pallas as pl
from jax.experimental.pallas import tpu as pltpu
from jax.sharding import PartitionSpec as P


MOMENTUM = 0.9
LEARN_RATE = 0.1
SUB, LANE = 8, 128
MIB = 1 << 20
STRIDE = SUB + 1
FETCH_BLOCKS, UNROLL, UNPACK_BLOCKS = 4, 16, 4
FIRST_MIB, FETCH_MIB, LATER_MIB = 58, 58, 28
F32, BF16 = jnp.float32, jnp.bfloat16
HALF_ROOT = 0.7071067811865476
PDF_SCALE = 0.3989422804014327


def table_copies(x_ref, y_ref, held, sems):
    count = x_ref.shape[0]
    block = count // FETCH_BLOCKS
    copies = []
    for part in range(FETCH_BLOCKS):
        place = pl.ds(part * block, block)
        for side, ref in enumerate((x_ref, y_ref)):
            copies.append(
                pltpu.make_async_copy(ref.at[place], held.at[side, place], sems.at[2 * part + side])
            )
    return copies


def build_table(copies, held, table):
    _, count, width = held.shape
    block, lanes = count // FETCH_BLOCKS, width // LANE
    for part in range(FETCH_BLOCKS):
        for side in range(2):
            copies[2 * part + side].wait()
            for lane in range(lanes):
                place = pl.ds(part * block * STRIDE + side * lanes + lane, block, stride=STRIDE)
                table[place, :] = held[
                    side, part * block : (part + 1) * block, lane * LANE : (lane + 1) * LANE
                ].astype(F32)


def pick_rows(picks_ref, step, visit_index, table, picked, outs, first):
    rows = picks_ref.shape[3]

    @pl.loop(0, rows // UNROLL)
    def _(group):
        for offset in range(UNROLL):
            row = group * UNROLL + offset
            pick = picks_ref[0, step, visit_index, row]
            picked[pl.ds(row * STRIDE, SUB), :] = table[pl.ds(pick * STRIDE, SUB), :]

    lanes = outs[0].shape[1] // LANE
    for side, ref in enumerate(outs):
        for lane in range(lanes):
            place = pl.ds(side * lanes + lane, rows, stride=STRIDE)
            ref[first : first + rows, lane * LANE : (lane + 1) * LANE] = picked[place, :].astype(
                ref.dtype
            )


def table_scratch(features, rows):
    count, width = features.shape
    if 2 * width > SUB * LANE or count % FETCH_BLOCKS or rows % UNROLL:
        raise ValueError("sizes")
    return [
        pltpu.VMEM((2, count, width), features.dtype),
        pltpu.VMEM((count * STRIDE, LANE), F32),
        pltpu.VMEM((rows * STRIDE, LANE), F32),
        pltpu.SemaphoreType.DMA((2 * FETCH_BLOCKS,)),
    ]


def fetch_kernel(visit_index, picks_ref, x_ref, y_ref, x_out, y_out, held, table, picked, sems):
    _, steps, _, rows = picks_ref.shape
    copies = table_copies(x_ref, y_ref, held, sems)
    for copy in copies:
        copy.start()
    build_table(copies, held, table)
    for step in range(steps):
        pick_rows(picks_ref, step, visit_index, table, picked, (x_out, y_out), step * rows)


def fetch(features, targets, picks, visit_index):
    count, width = features.shape
    _, steps, _, rows = picks.shape
    return pl.pallas_call(
        functools.partial(fetch_kernel, visit_index),
        in_specs=[SCALARS, ANYWHERE, ANYWHERE],
        out_specs=[pl.BlockSpec(memory_space=pltpu.VMEM)] * 2,
        out_shape=[jax.ShapeDtypeStruct((steps * rows, width), features.dtype)] * 2,
        scratch_shapes=table_scratch(features, rows),
        compiler_params=pltpu.CompilerParams(vmem_limit_bytes=FETCH_MIB * MIB),
        cost_estimate=pl.CostEstimate(
            flops=0, bytes_accessed=4 * count * width, transcendentals=0
        ),
        name="fetch",
    )(picks, features, targets)


def tiles_of(shape):
    rows, cols = shape[-2:]
    return [
        (row * SUB, col * LANE) for row in range(rows // SUB) for col in range(cols // LANE)
    ]


def tile_slots(shapes, devices):
    slots, base = [], 0
    for shape in shapes:
        tiles = tiles_of(shape)
        if len(tiles) % devices:
            raise ValueError("uneven tiles")
        each = len(tiles) // devices
        slots.append(
            [(index // each, base + index % each, *tile) for index, tile in enumerate(tiles)]
        )
        base += each
    return slots, base


def pack(refs, slots, packed_ref):
    for ref, places in zip(refs, slots):
        for chunk, slot, row, col in places:
            packed_ref[chunk, slot] = ref[row : row + SUB, col : col + LANE].astype(
                packed_ref.dtype
            )


def unpack(packed_ref, slots, refs):
    for ref, places in zip(refs, slots):
        for chunk, slot, row, col in places:
            ref[row : row + SUB, col : col + LANE] = packed_ref[chunk, slot].astype(ref.dtype)


def collect(me_ref, piece_refs, packed_ref, sems):
    chip = me_ref[0] // 2
    return [
        pltpu.make_async_copy(ref, packed_ref.at[chip ^ k], sems.at[k])
        for k, ref in enumerate(piece_refs)
    ]


def scatter(me_ref, packed_ref, piece_refs, sems):
    chip = me_ref[0] // 2
    return [
        pltpu.make_async_copy(packed_ref.at[chip ^ k], ref, sems.at[k])
        for k, ref in enumerate(piece_refs)
    ]


def train_step(x_ref, y_ref, win, wout, min_, mout, hid, dout, dpre, block):
    rows = x_ref.shape[0]
    cast_in = win[...].astype(BF16)
    cast_out = wout[...].astype(BF16)
    for start in range(0, rows, block):
        part = slice(start, start + block)
        batch_x = x_ref[part, :]
        preact = jnp.dot(batch_x, cast_in, preferred_element_type=F32)
        cdf = 0.5 * (1.0 + lax.erf(preact * HALF_ROOT))
        pdf = PDF_SCALE * jnp.exp(-0.5 * preact * preact)
        hidden = (preact * cdf).astype(BF16)
        hid[part, :] = hidden
        error = (
            batch_x.astype(F32)
            + jnp.dot(hidden, cast_out, preferred_element_type=F32)
            - y_ref[part, :].astype(F32)
        )
        d_out = (error * (1.0 / rows)).astype(BF16)
        dout[part, :] = d_out
        d_hidden = lax.dot_general(
            d_out, cast_out, (((1,), (1,)), ((), ())), preferred_element_type=F32
        )
        dpre[part, :] = (d_hidden * (cdf + preact * pdf)).astype(BF16)
    over_rows = (((0,), (0,)), ((), ()))
    grad = lax.dot_general(hid[...], dout[...], over_rows, preferred_element_type=F32)
    moment = (MOMENTUM * mout[...].astype(F32) + grad).astype(BF16)
    mout[...] = moment
    wout[...] = wout[...] - LEARN_RATE * moment.astype(F32)
    grad = lax.dot_general(x_ref[...], dpre[...], over_rows, preferred_element_type=F32)
    moment = (MOMENTUM * min_[...].astype(F32) + grad).astype(BF16)
    min_[...] = moment
    win[...] = win[...] - LEARN_RATE * moment.astype(F32)


def send_out(slots, pieces, me_ref, state, refs, packed, sems):
    weights_ref, moment_refs = refs[0], refs[1:]
    pack(state[2:], slots[pieces], packed)
    copies = scatter(me_ref, packed, moment_refs, sems)
    for copy in copies:
        copy.start()
    pack(state[:2], slots[2 * pieces], weights_ref)
    for copy in copies:
        copy.wait()


def later_visit_kernel(slots, pieces, block, me_ref, x_ref, y_ref, weights_ref, *refs):
    moment_refs, sent, scratch = refs[:pieces], refs[pieces:][: pieces + 1], refs[2 * pieces + 1 :]
    state, work, (packed, sems) = scratch[:4], scratch[4:7], scratch[7:9]
    step = pl.program_id(0)

    @pl.when(step == 0)
    def _():
        copies = collect(me_ref, moment_refs, packed, sems)
        for copy in copies:
            copy.start()
        unpack(weights_ref, slots[2 * pieces], state[:2])
        for copy in copies:
            copy.wait()
        unpack(packed, slots[pieces], state[2:])

    train_step(x_ref, y_ref, *state, *work, block)

    @pl.when(step == pl.num_programs(0) - 1)
    def _():
        send_out(slots, pieces, me_ref, state, sent, packed, sems)


def first_visit_kernel(slots, pieces, block, me_ref, picks_ref, x_ref, y_ref, *refs):
    model, sent, scratch = refs[:4], refs[4:][: pieces + 1], refs[pieces + 5 :]
    state, work, (packed, packed_sems) = scratch[:4], scratch[4:7], scratch[7:9]
    batch = scratch[9:11]
    held, table, picked, sems, model_sems = scratch[11:]
    step = pl.program_id(0)

    @pl.when(step == 0)
    def _():
        copies = table_copies(x_ref, y_ref, held, sems)
        loads = [
            pltpu.make_async_copy(ref, kept, model_sems.at[index])
            for index, (ref, kept) in enumerate(zip(model, state))
        ]
        for copy in copies + loads:
            copy.start()
        build_table(copies, held, table)
        for copy in loads:
            copy.wait()

    pick_rows(picks_ref, step, 0, table, picked, batch, 0)
    train_step(*batch, *state, *work, block)

    @pl.when(step == pl.num_programs(0) - 1)
    def _():
        send_out(slots, pieces, me_ref, state, sent, packed, packed_sems)


def whole(shape):
    return pl.BlockSpec(shape, lambda step: (0,) * len(shape))


SCALARS = pl.BlockSpec(memory_space=pltpu.SMEM)
ANYWHERE = pl.BlockSpec(memory_space=pl.ANY)


def visit(kernel, args, in_specs, more_scratch, limit, sizes, slots):
    steps, rows, width, hidden = sizes
    pieces = min(slots)
    depth = 2 * width * hidden // (SUB * LANE)
    piece_shape = (depth // pieces, SUB, LANE)
    packed_shape = (2 * pieces, depth // (2 * pieces), SUB, LANE)
    outs = pl.pallas_call(
        functools.partial(kernel, slots, pieces, rows // 4),
        grid=(steps,),
        in_specs=in_specs,
        out_specs=[whole(packed_shape)] + [ANYWHERE] * pieces,
        out_shape=[jax.ShapeDtypeStruct(packed_shape, BF16)]
        + [jax.ShapeDtypeStruct(piece_shape, BF16)] * pieces,
        scratch_shapes=[
            pltpu.VMEM((width, hidden), F32),
            pltpu.VMEM((hidden, width), F32),
            pltpu.VMEM((width, hidden), BF16),
            pltpu.VMEM((hidden, width), BF16),
            pltpu.VMEM((rows, hidden), BF16),
            pltpu.VMEM((rows, width), BF16),
            pltpu.VMEM((rows, hidden), BF16),
            pltpu.VMEM((pieces, *piece_shape), BF16),
            pltpu.SemaphoreType.DMA((pieces,)),
            *more_scratch,
        ],
        cost_estimate=pl.CostEstimate(
            flops=steps * 10 * rows * width * hidden,
            bytes_accessed=4 * steps * rows * width + 32 * width * hidden,
            transcendentals=2 * steps * rows * hidden,
        ),
        compiler_params=pltpu.CompilerParams(vmem_limit_bytes=limit * MIB),
        name="visit",
    )(*args)
    return outs[0], outs[1:]


def first_visit(me, features, targets, picks, model, sizes, slots):
    _, rows, width, _ = sizes
    scratch = [pltpu.VMEM((rows, width), BF16)] * 2 + table_scratch(features, rows)
    return visit(
        first_visit_kernel,
        (me, picks, features, targets, *model),
        [SCALARS] * 2 + [ANYWHERE] * 6,
        scratch + [pltpu.SemaphoreType.DMA((4,))],
        FIRST_MIB,
        sizes,
        slots,
    )


def later_visit(me, batch, weights, moments, sizes, slots):
    _, rows, width, _ = sizes
    batch_spec = pl.BlockSpec((rows, width), lambda step: (step, 0))
    return visit(
        later_visit_kernel,
        (me, *batch, weights, *moments),
        [SCALARS, batch_spec, batch_spec, whole(weights.shape)] + [ANYWHERE] * len(moments),
        [],
        LATER_MIB,
        sizes,
        slots,
    )


def reorder_kernel(source_ref, packed_ref, out_ref, sems):
    copies = [
        pltpu.make_async_copy(packed_ref.at[source_ref[slot]], out_ref.at[slot], sems.at[slot])
        for slot in range(out_ref.shape[0])
    ]
    for copy in copies:
        copy.start()
    for copy in copies:
        copy.wait()


def reorder(packed, source):
    return pl.pallas_call(
        reorder_kernel,
        in_specs=[
            pl.BlockSpec(memory_space=pltpu.SMEM),
            pl.BlockSpec(memory_space=pltpu.VMEM),
        ],
        out_specs=pl.BlockSpec(memory_space=pl.ANY),
        out_shape=jax.ShapeDtypeStruct(packed.shape, packed.dtype),
        scratch_shapes=[pltpu.SemaphoreType.DMA((packed.shape[0],))],
        compiler_params=pltpu.CompilerParams(vmem_limit_bytes=8 * MIB),
        name="reorder",
    )(source, packed)


def unpack_blocks(packed, outs, devices):
    blocks = UNPACK_BLOCKS if devices % UNPACK_BLOCKS == 0 else 1
    parts = [(shape[0] // blocks, shape[1]) for shape, _ in outs]
    slots, _ = tile_slots(parts, devices // blocks)
    return pl.pallas_call(
        functools.partial(unpack_kernel, slots),
        grid=(blocks,),
        in_specs=[
            pl.BlockSpec((devices // blocks, *packed.shape[1:]), lambda block: (block, 0, 0, 0))
        ],
        out_specs=[pl.BlockSpec(part, lambda block: (block, 0)) for part in parts],
        out_shape=[jax.ShapeDtypeStruct(shape, dtype) for shape, dtype in outs],
        compiler_params=pltpu.CompilerParams(vmem_limit_bytes=16 * MIB),
        name="unpack",
    )(packed)


def stack_kernel(*refs):
    parts, out_ref, sems = refs[:-2], refs[-2], refs[-1]
    copies = [
        pltpu.make_async_copy(ref, out_ref.at[k], sems.at[k]) for k, ref in enumerate(parts)
    ]
    for copy in copies:
        copy.start()
    for copy in copies:
        copy.wait()


def stacked(parts):
    shape = (len(parts), *parts[0].shape)
    return pl.pallas_call(
        stack_kernel,
        in_specs=[ANYWHERE] * len(parts),
        out_specs=pl.BlockSpec(memory_space=pltpu.VMEM),
        out_shape=jax.ShapeDtypeStruct(shape, parts[0].dtype),
        scratch_shapes=[pltpu.SemaphoreType.DMA((len(parts),))],
        compiler_params=pltpu.CompilerParams(vmem_limit_bytes=8 * MIB),
        name="stack",
    )(*parts)


def route_kernel(pieces, me_ref, source_ref, own_ref, partner_ref, *refs):
    out_refs, sems = refs[:pieces], refs[pieces]
    chip, core = me_ref[0] // 2, me_ref[0] % 2
    for k, out_ref in enumerate(out_refs):
        source = source_ref[2 * (chip ^ k) + core]
        place = chip ^ (source // 2)

        @pl.when(source % 2 == core)
        def _():
            pltpu.make_async_copy(own_ref.at[place], out_ref, sems.at[k]).start()

        @pl.when(source % 2 != core)
        def _():
            pltpu.make_async_copy(partner_ref.at[place], out_ref, sems.at[k]).start()

    for k, out_ref in enumerate(out_refs):
        pltpu.make_async_copy(own_ref.at[0], out_ref, sems.at[k]).wait()


def route(me, source, own, partner):
    pieces = own.shape[0]
    in_vmem = pl.BlockSpec(memory_space=pltpu.VMEM)
    return pl.pallas_call(
        functools.partial(route_kernel, pieces),
        in_specs=[SCALARS, SCALARS, in_vmem, in_vmem],
        out_specs=[ANYWHERE] * pieces,
        out_shape=[jax.ShapeDtypeStruct(own.shape[1:], own.dtype)] * pieces,
        scratch_shapes=[pltpu.SemaphoreType.DMA((pieces,))],
        cost_estimate=pl.CostEstimate(
            flops=0, bytes_accessed=4 * own.size, transcendentals=0
        ),
        compiler_params=pltpu.CompilerParams(vmem_limit_bytes=8 * MIB),
        name="route",
    )(me, source, own, partner)


def unpack_pieces_kernel(slots, pieces, me_ref, *refs):
    given, outs, (packed, sems) = refs[:pieces], refs[pieces:-2], refs[-2:]
    copies = collect(me_ref, given, packed, sems)
    for copy in copies:
        copy.start()
    for copy in copies:
        copy.wait()
    unpack(packed, slots, outs)


def unpack_pieces(me, given, slots, outs):
    pieces = len(given)
    return pl.pallas_call(
        functools.partial(unpack_pieces_kernel, slots, pieces),
        in_specs=[SCALARS] + [ANYWHERE] * pieces,
        out_specs=[pl.BlockSpec(memory_space=pltpu.VMEM)] * len(outs),
        out_shape=[jax.ShapeDtypeStruct(shape, dtype) for shape, dtype in outs],
        scratch_shapes=[
            pltpu.VMEM((pieces, *given[0].shape), BF16),
            pltpu.SemaphoreType.DMA((pieces,)),
        ],
        compiler_params=pltpu.CompilerParams(vmem_limit_bytes=16 * MIB),
        name="unpack",
    )(me, *given)


def unpack_kernel(slots, packed_ref, *out_refs):
    unpack(packed_ref, slots, out_refs)


def invert(order):
    count = order.shape[0]
    places = jnp.arange(count, dtype=jnp.int32)
    matches = order[:, None] == places[None, :]
    return jnp.sum(jnp.where(matches, places[:, None], 0), axis=0).astype(jnp.int32)


def exchange(packed):
    return lax.all_to_all(packed, "hop", split_axis=0, concat_axis=0, tiled=True)


def spread(parts, devices):
    moved = [None] * len(parts)
    moved[0] = parts[0]
    for k in sorted(range(1, len(parts)), reverse=True):
        moved[k] = lax.ppermute(parts[k], "hop", [(i, i ^ (2 * k)) for i in range(devices)])
    return moved


def move(weights, moments, me, source, devices, beside=()):
    weights = exchange(weights)
    moments = spread(moments, devices)
    if beside:
        weights, *beside = lax.optimization_barrier((weights, *beside))
    weights = reorder(weights, source)
    weights = exchange(weights)
    own = stacked(moments)
    partner = lax.ppermute(own, "hop", [(i, i ^ 1) for i in range(devices)])
    moments = route(me, source, own, partner)
    moments = spread(moments, devices)
    return weights, moments, beside


def on_device(
    features, targets, row_index, hop_order, weight_in, weight_out, moment_in, moment_out
):
    devices = lax.axis_size("hop")
    me = lax.axis_index("hop").astype(jnp.int32).reshape(1)
    model = (weight_in[0], weight_out[0], moment_in[0], moment_out[0])
    outs = [(member.shape, member.dtype) for member in model]
    shapes = [member.shape for member in model[:2]]
    pieces = devices // 2
    slots = {count: tile_slots(shapes, count)[0] for count in (pieces, devices)}
    _, visits, steps, rows = row_index.shape
    sizes = (steps, rows, *shapes[0])
    picks = jnp.transpose(row_index, (0, 2, 1, 3))
    sources = [invert(hop_order[visit_index]) for visit_index in range(visits)]
    weights, moments = first_visit(me, features, targets, picks, model, sizes, slots)
    for visit_index in range(1, visits):
        batch = fetch(features, targets, picks, visit_index)
        weights, moments, batch = move(
            weights, moments, me, sources[visit_index - 1], devices, batch
        )
        weights, moments = later_visit(me, batch, weights, moments, sizes, slots)
    weights, moments, _ = move(weights, moments, me, sources[-1], devices)
    weights = unpack_blocks(weights, outs[:2], devices)
    moments = unpack_pieces(me, moments, slots[pieces], outs[2:])
    return tuple(member[None] for member in (*weights, *moments))


def solution(mesh):
    split = P(("groups", "hop"), None, None)
    in_specs = (
        P(("groups", "hop"), None),
        P(("groups", "hop"), None),
        P(("groups", "hop"), None, None, None),
        P("groups", None),
        split,
        split,
        split,
        split,
    )
    return jax.shard_map(
        on_device, mesh=mesh, in_specs=in_specs, out_specs=(split,) * 4, check_vma=False
    )
```

```python
import functools

import jax
import jax.numpy as jnp
from jax import lax
from jax.experimental import pallas as pl
from jax.experimental.pallas import tpu as pltpu
from jax.sharding import PartitionSpec as P


MOMENTUM = 0.9
LEARN_RATE = 0.1
SUB, LANE = 8, 128
MIB = 1 << 20
STRIDE = SUB + 1
FETCH_BLOCKS, UNROLL = 4, 32
FIRST_MIB, FETCH_MIB, LATER_MIB, LAST_MIB, SETTLE_MIB = 58, 58, 58, 58, 16
F32, BF16 = jnp.float32, jnp.bfloat16
HALF_ROOT = 0.7071067811865476
PDF_SCALE = 0.3989422804014327


def table_copies(x_ref, y_ref, held, sems):
    count = x_ref.shape[0]
    block = count // FETCH_BLOCKS
    copies = []
    for part in range(FETCH_BLOCKS):
        place = pl.ds(part * block, block)
        for side, ref in enumerate((x_ref, y_ref)):
            copies.append(
                pltpu.make_async_copy(ref.at[place], held.at[side, place], sems.at[2 * part + side])
            )
    return copies


def build_table(copies, held, table):
    _, count, width = held.shape
    block, lanes = count // FETCH_BLOCKS, width // LANE
    for part in range(FETCH_BLOCKS):
        for side in range(2):
            copies[2 * part + side].wait()
            for lane in range(lanes):
                place = pl.ds(part * block * STRIDE + side * lanes + lane, block, stride=STRIDE)
                table[place, :] = held[
                    side, part * block : (part + 1) * block, lane * LANE : (lane + 1) * LANE
                ].astype(F32)


def pick_rows(picks_ref, step, visit_index, table, picked, outs, first):
    rows = picks_ref.shape[3]

    @pl.loop(0, rows // UNROLL)
    def _(group):
        for offset in range(UNROLL):
            row = group * UNROLL + offset
            pick = picks_ref[0, step, visit_index, row]
            picked[pl.ds(row * STRIDE, SUB), :] = table[pl.ds(pick * STRIDE, SUB), :]

    lanes = outs[0].shape[1] // LANE
    for side, ref in enumerate(outs):
        for lane in range(lanes):
            place = pl.ds(side * lanes + lane, rows, stride=STRIDE)
            ref[first : first + rows, lane * LANE : (lane + 1) * LANE] = picked[place, :].astype(
                ref.dtype
            )


def table_scratch(features, rows):
    count, width = features.shape
    if 2 * width > SUB * LANE or count % FETCH_BLOCKS or rows % UNROLL:
        raise ValueError("sizes")
    return [
        pltpu.VMEM((2, count, width), features.dtype),
        pltpu.VMEM((count * STRIDE, LANE), F32),
        pltpu.VMEM((rows * STRIDE, LANE), F32),
        pltpu.SemaphoreType.DMA((2 * FETCH_BLOCKS,)),
    ]


def fetch_kernel(visit_index, picks_ref, x_ref, y_ref, x_out, y_out, held, table, picked, sems):
    _, steps, _, rows = picks_ref.shape
    copies = table_copies(x_ref, y_ref, held, sems)
    for copy in copies:
        copy.start()
    build_table(copies, held, table)
    for step in range(steps):
        pick_rows(picks_ref, step, visit_index, table, picked, (x_out, y_out), step * rows)


def fetch(features, targets, picks, visit_index):
    count, width = features.shape
    _, steps, _, rows = picks.shape
    return pl.pallas_call(
        functools.partial(fetch_kernel, visit_index),
        in_specs=[SCALARS, ANYWHERE, ANYWHERE],
        out_specs=[pl.BlockSpec(memory_space=pltpu.VMEM)] * 2,
        out_shape=[jax.ShapeDtypeStruct((steps * rows, width), features.dtype)] * 2,
        scratch_shapes=table_scratch(features, rows),
        compiler_params=pltpu.CompilerParams(vmem_limit_bytes=FETCH_MIB * MIB),
        cost_estimate=pl.CostEstimate(
            flops=0, bytes_accessed=4 * count * width, transcendentals=0
        ),
        name="fetch",
    )(picks, features, targets)


def tiles_of(shape):
    rows, cols = shape[-2:]
    return [
        (row * SUB, col * LANE) for row in range(rows // SUB) for col in range(cols // LANE)
    ]


def tile_slots(shapes, devices):
    slots, base = [], 0
    for shape in shapes:
        tiles = tiles_of(shape)
        if len(tiles) % devices:
            raise ValueError("uneven tiles")
        each = len(tiles) // devices
        slots.append(
            [(index // each, base + index % each, *tile) for index, tile in enumerate(tiles)]
        )
        base += each
    return slots, base


def pack(refs, slots, packed_ref):
    for ref, places in zip(refs, slots):
        for chunk, slot, row, col in places:
            packed_ref[chunk, slot] = ref[row : row + SUB, col : col + LANE].astype(
                packed_ref.dtype
            )


def unpack(packed_ref, slots, refs):
    for ref, places in zip(refs, slots):
        for chunk, slot, row, col in places:
            ref[row : row + SUB, col : col + LANE] = packed_ref[chunk, slot].astype(ref.dtype)


def collect(me_ref, piece_refs, packed_ref, sems):
    chip = me_ref[0] // 2
    return [
        pltpu.make_async_copy(ref, packed_ref.at[chip ^ k], sems.at[k])
        for k, ref in enumerate(piece_refs)
    ]


def scatter(me_ref, packed_ref, piece_refs, sems):
    chip = me_ref[0] // 2
    return [
        pltpu.make_async_copy(packed_ref.at[chip ^ k], ref, sems.at[k])
        for k, ref in enumerate(piece_refs)
    ]


def gradients(x_ref, y_ref, cast_in, cast_out, hid, dout, dpre, block):
    rows = x_ref.shape[0]
    for start in range(0, rows, block):
        part = slice(start, start + block)
        batch_x = x_ref[part, :]
        preact = jnp.dot(batch_x, cast_in, preferred_element_type=F32)
        cdf = 0.5 * (1.0 + lax.erf(preact * HALF_ROOT))
        pdf = PDF_SCALE * jnp.exp(-0.5 * preact * preact)
        hidden = (preact * cdf).astype(BF16)
        hid[part, :] = hidden
        error = (
            batch_x.astype(F32)
            + jnp.dot(hidden, cast_out, preferred_element_type=F32)
            - y_ref[part, :].astype(F32)
        )
        d_out = (error * (1.0 / rows)).astype(BF16)
        dout[part, :] = d_out
        d_hidden = lax.dot_general(
            d_out, cast_out, (((1,), (1,)), ((), ())), preferred_element_type=F32
        )
        dpre[part, :] = (d_hidden * (cdf + preact * pdf)).astype(BF16)


OVER_ROWS = (((0,), (0,)), ((), ()))


def momentum_in(x_ref, dpre, moment):
    grad = lax.dot_general(x_ref[...], dpre[...], OVER_ROWS, preferred_element_type=F32)
    return (MOMENTUM * moment[...].astype(F32) + grad).astype(BF16)


def momentum_out(hid, dout, moment):
    grad = lax.dot_general(hid[...], dout[...], OVER_ROWS, preferred_element_type=F32)
    return (MOMENTUM * moment[...].astype(F32) + grad).astype(BF16)


def stepped(weight, moment):
    return weight - LEARN_RATE * moment.astype(F32)


def train_step(x_ref, y_ref, win, wout, min_, mout, hid, dout, dpre, block):
    cast_in, cast_out = win[...].astype(BF16), wout[...].astype(BF16)
    gradients(x_ref, y_ref, cast_in, cast_out, hid, dout, dpre, block)
    moment = momentum_out(hid, dout, mout)
    mout[...] = moment
    wout[...] = stepped(wout[...], moment)
    moment = momentum_in(x_ref, dpre, min_)
    min_[...] = moment
    win[...] = stepped(win[...], moment)


def hand_over(slots, pieces, state, sent):
    packed, kept = sent[0], sent[1:5]
    pack(state[:2], slots[2 * pieces], packed)
    for ref, held in zip(kept, state):
        ref[...] = held[...].astype(BF16)


def later_visit_kernel(slots, pieces, block, me_ref, x_ref, y_ref, weights_ref, *refs):
    moment_refs, sent, scratch = refs[:pieces], refs[pieces:][:5], refs[pieces + 5 :]
    state, work, (packed, sems) = scratch[:4], scratch[4:7], scratch[7:9]
    step = pl.program_id(0)

    @pl.when(step == 0)
    def _():
        copies = collect(me_ref, moment_refs, packed, sems)
        for copy in copies:
            copy.start()
        unpack(weights_ref, slots[2 * pieces], state[:2])
        for copy in copies:
            copy.wait()
        unpack(packed, slots[pieces], state[2:])
        for weight, moment in zip(state[:2], state[2:]):
            weight[...] = stepped(weight[...], moment[...])

    train_step(x_ref, y_ref, *state, *work, block)

    @pl.when(step == pl.num_programs(0) - 1)
    def _():
        hand_over(slots, pieces, state, sent)


def first_visit_kernel(slots, pieces, block, picks_ref, x_ref, y_ref, *refs):
    model, sent, scratch = refs[:4], refs[4:11], refs[11:]
    state, work, batch = scratch[:4], scratch[4:7], scratch[7:9]
    held, table, picked, sems, model_sems = scratch[9:]
    step = pl.program_id(0)

    @pl.when(step == 0)
    def _():
        copies = table_copies(x_ref, y_ref, held, sems)
        loads = [
            pltpu.make_async_copy(ref, kept, model_sems.at[index])
            for index, (ref, kept) in enumerate(zip(model, state))
        ]
        for copy in copies + loads:
            copy.start()
        build_table(copies, held, table)
        for copy in loads:
            copy.wait()

    pick_rows(picks_ref, step, 0, table, picked, batch, 0)
    train_step(*batch, *state, *work, block)

    @pl.when(step == pl.num_programs(0) - 1)
    def _():
        hand_over(slots, pieces, state, sent)
        pick_rows(picks_ref, step + 1, 0, table, picked, sent[5:], 0)


def last_step_kernel(slots, pieces, block, me_ref, x_ref, y_ref, *refs):
    cast_in, cast_out, min_, mout = refs[:4]
    moment_refs, (hid, dout, dpre, new_in, new_out, packed, sems) = refs[4:-7], refs[-7:]
    gradients(x_ref, y_ref, cast_in[...], cast_out[...], hid, dout, dpre, block)
    new_out[...] = momentum_out(hid, dout, mout)
    new_in[...] = momentum_in(x_ref, dpre, min_)
    pack((new_in, new_out), slots[pieces], packed)
    copies = scatter(me_ref, packed, moment_refs, sems)
    for copy in copies:
        copy.start()
    for copy in copies:
        copy.wait()


def whole(shape):
    return pl.BlockSpec(shape, lambda step: (0,) * len(shape))


SCALARS = pl.BlockSpec(memory_space=pltpu.SMEM)
ANYWHERE = pl.BlockSpec(memory_space=pl.ANY)


def work_scratch(rows, width, hidden):
    return [
        pltpu.VMEM((rows, hidden), BF16),
        pltpu.VMEM((rows, width), BF16),
        pltpu.VMEM((rows, hidden), BF16),
    ]


def step_cost(steps, rows, width, hidden):
    return pl.CostEstimate(
        flops=steps * 10 * rows * width * hidden,
        bytes_accessed=4 * steps * rows * width + 16 * width * hidden,
        transcendentals=2 * steps * rows * hidden,
    )


def visit(kernel, args, in_specs, more_outs, more_scratch, limit, sizes, slots):
    steps, rows, width, hidden = sizes
    pieces = min(slots)
    depth = 2 * width * hidden // (SUB * LANE)
    packed_shape = (2 * pieces, depth // (2 * pieces), SUB, LANE)
    shapes = [packed_shape] + [(width, hidden), (hidden, width)] * 2 + more_outs
    return pl.pallas_call(
        functools.partial(kernel, slots, pieces, rows // 4),
        grid=(steps - 1,),
        in_specs=in_specs,
        out_specs=[whole(shape) for shape in shapes],
        out_shape=[jax.ShapeDtypeStruct(shape, BF16) for shape in shapes],
        scratch_shapes=[
            pltpu.VMEM((width, hidden), F32),
            pltpu.VMEM((hidden, width), F32),
            pltpu.VMEM((width, hidden), BF16),
            pltpu.VMEM((hidden, width), BF16),
            *work_scratch(rows, width, hidden),
            *more_scratch,
        ],
        cost_estimate=step_cost(steps - 1, rows, width, hidden),
        compiler_params=pltpu.CompilerParams(vmem_limit_bytes=limit * MIB),
        name="visit",
    )(*args)


def first_visit(features, targets, picks, model, sizes, slots):
    _, rows, width, _ = sizes
    scratch = [pltpu.VMEM((rows, width), BF16)] * 2 + table_scratch(features, rows)
    outs = visit(
        first_visit_kernel,
        (picks, features, targets, *model),
        [SCALARS] + [ANYWHERE] * 6,
        [(rows, width)] * 2,
        scratch + [pltpu.SemaphoreType.DMA((4,))],
        FIRST_MIB,
        sizes,
        slots,
    )
    return outs[0], outs[1:5], outs[5:]


def piece_scratch(pieces, piece_shape):
    return [pltpu.VMEM((pieces, *piece_shape), BF16), pltpu.SemaphoreType.DMA((pieces,))]


def later_visit(me, batch, weights, moments, sizes, slots):
    _, rows, width, _ = sizes
    batch_spec = pl.BlockSpec((rows, width), lambda step: (step, 0))
    outs = visit(
        later_visit_kernel,
        (me, *batch, weights, *moments),
        [SCALARS, batch_spec, batch_spec, whole(weights.shape)] + [ANYWHERE] * len(moments),
        [],
        piece_scratch(len(moments), moments[0].shape),
        LATER_MIB,
        sizes,
        slots,
    )
    return outs[0], outs[1:]


def last_step(me, batch, kept, sizes, slots):
    _, rows, width, hidden = sizes
    pieces = min(slots)
    piece_shape = (2 * width * hidden // (SUB * LANE) // pieces, SUB, LANE)
    last = batch[0].shape[0] // rows - 1
    batch_spec = pl.BlockSpec((rows, width), lambda step: (last, 0))
    return pl.pallas_call(
        functools.partial(last_step_kernel, slots, pieces, rows // 4),
        grid=(1,),
        in_specs=[SCALARS, batch_spec, batch_spec] + [whole(part.shape) for part in kept],
        out_specs=[ANYWHERE] * pieces,
        out_shape=[jax.ShapeDtypeStruct(piece_shape, BF16)] * pieces,
        scratch_shapes=[
            *work_scratch(rows, width, hidden),
            pltpu.VMEM((width, hidden), BF16),
            pltpu.VMEM((hidden, width), BF16),
            *piece_scratch(pieces, piece_shape),
        ],
        cost_estimate=step_cost(1, rows, width, hidden),
        compiler_params=pltpu.CompilerParams(vmem_limit_bytes=LAST_MIB * MIB),
        name="last",
    )(me, *batch, *kept)


def reorder_kernel(source_ref, packed_ref, out_ref, sems):
    copies = [
        pltpu.make_async_copy(packed_ref.at[source_ref[slot]], out_ref.at[slot], sems.at[slot])
        for slot in range(out_ref.shape[0])
    ]
    for copy in copies:
        copy.start()
    for copy in copies:
        copy.wait()


def reorder(packed, source):
    return pl.pallas_call(
        reorder_kernel,
        in_specs=[
            pl.BlockSpec(memory_space=pltpu.SMEM),
            pl.BlockSpec(memory_space=pltpu.VMEM),
        ],
        out_specs=pl.BlockSpec(memory_space=pl.ANY),
        out_shape=jax.ShapeDtypeStruct(packed.shape, packed.dtype),
        scratch_shapes=[pltpu.SemaphoreType.DMA((packed.shape[0],))],
        compiler_params=pltpu.CompilerParams(vmem_limit_bytes=8 * MIB),
        name="reorder",
    )(source, packed)


def stack_kernel(*refs):
    parts, out_ref, sems = refs[:-2], refs[-2], refs[-1]
    copies = [
        pltpu.make_async_copy(ref, out_ref.at[k], sems.at[k]) for k, ref in enumerate(parts)
    ]
    for copy in copies:
        copy.start()
    for copy in copies:
        copy.wait()


def stacked(parts):
    shape = (len(parts), *parts[0].shape)
    return pl.pallas_call(
        stack_kernel,
        in_specs=[ANYWHERE] * len(parts),
        out_specs=pl.BlockSpec(memory_space=pltpu.VMEM),
        out_shape=jax.ShapeDtypeStruct(shape, parts[0].dtype),
        scratch_shapes=[pltpu.SemaphoreType.DMA((len(parts),))],
        compiler_params=pltpu.CompilerParams(vmem_limit_bytes=8 * MIB),
        name="stack",
    )(*parts)


def route_kernel(pieces, me_ref, source_ref, own_ref, partner_ref, *refs):
    out_refs, sems = refs[:pieces], refs[pieces]
    chip, core = me_ref[0] // 2, me_ref[0] % 2
    for k, out_ref in enumerate(out_refs):
        source = source_ref[2 * (chip ^ k) + core]
        place = chip ^ (source // 2)

        @pl.when(source % 2 == core)
        def _():
            pltpu.make_async_copy(own_ref.at[place], out_ref, sems.at[k]).start()

        @pl.when(source % 2 != core)
        def _():
            pltpu.make_async_copy(partner_ref.at[place], out_ref, sems.at[k]).start()

    for k, out_ref in enumerate(out_refs):
        pltpu.make_async_copy(own_ref.at[0], out_ref, sems.at[k]).wait()


def route(me, source, own, partner):
    pieces = own.shape[0]
    in_vmem = pl.BlockSpec(memory_space=pltpu.VMEM)
    return pl.pallas_call(
        functools.partial(route_kernel, pieces),
        in_specs=[SCALARS, SCALARS, in_vmem, in_vmem],
        out_specs=[ANYWHERE] * pieces,
        out_shape=[jax.ShapeDtypeStruct(own.shape[1:], own.dtype)] * pieces,
        scratch_shapes=[pltpu.SemaphoreType.DMA((pieces,))],
        cost_estimate=pl.CostEstimate(
            flops=0, bytes_accessed=4 * own.size, transcendentals=0
        ),
        compiler_params=pltpu.CompilerParams(vmem_limit_bytes=8 * MIB),
        name="route",
    )(me, source, own, partner)


def settle_kernel(slots, pieces, me_ref, weights_ref, *refs):
    moment_refs, outs, (packed, sems) = refs[:pieces], refs[pieces:-2], refs[-2:]
    copies = collect(me_ref, moment_refs, packed, sems)
    for copy in copies:
        copy.start()
    unpack(weights_ref, slots[2 * pieces], outs[:2])
    for copy in copies:
        copy.wait()
    unpack(packed, slots[pieces], outs[2:])
    for weight, moment in zip(outs[:2], outs[2:]):
        weight[...] = stepped(weight[...], moment[...])


def settle(me, weights, moments, slots, outs):
    in_vmem = pl.BlockSpec(memory_space=pltpu.VMEM)
    return pl.pallas_call(
        functools.partial(settle_kernel, slots, len(moments)),
        in_specs=[SCALARS, in_vmem] + [ANYWHERE] * len(moments),
        out_specs=[in_vmem] * len(outs),
        out_shape=[jax.ShapeDtypeStruct(shape, dtype) for shape, dtype in outs],
        scratch_shapes=piece_scratch(len(moments), moments[0].shape),
        compiler_params=pltpu.CompilerParams(vmem_limit_bytes=SETTLE_MIB * MIB),
        name="settle",
    )(me, weights, *moments)


def invert(order):
    count = order.shape[0]
    places = jnp.arange(count, dtype=jnp.int32)
    matches = order[:, None] == places[None, :]
    return jnp.sum(jnp.where(matches, places[:, None], 0), axis=0).astype(jnp.int32)


def exchange(packed):
    return lax.all_to_all(packed, "hop", split_axis=0, concat_axis=0, tiled=True)


def spread(parts, devices):
    moved = [None] * len(parts)
    moved[0] = parts[0]
    for k in sorted(range(1, len(parts)), reverse=True):
        moved[k] = lax.ppermute(parts[k], "hop", [(i, i ^ (2 * k)) for i in range(devices)])
    return moved


def move(weights, me, batch, kept, source, devices, sizes, slots):
    weights = exchange(weights)
    moments = last_step(me, batch, kept, sizes, slots)
    moments = spread(moments, devices)
    weights = reorder(weights, source)
    weights = exchange(weights)
    own = stacked(moments)
    partner = lax.ppermute(own, "hop", [(i, i ^ 1) for i in range(devices)])
    moments = route(me, source, own, partner)
    moments = spread(moments, devices)
    return weights, moments


def on_device(
    features, targets, row_index, hop_order, weight_in, weight_out, moment_in, moment_out
):
    devices = lax.axis_size("hop")
    me = lax.axis_index("hop").astype(jnp.int32).reshape(1)
    model = (weight_in[0], weight_out[0], moment_in[0], moment_out[0])
    outs = [(member.shape, member.dtype) for member in model]
    shapes = [member.shape for member in model[:2]]
    slots = {count: tile_slots(shapes, count)[0] for count in (devices // 2, devices)}
    _, visits, steps, rows = row_index.shape
    sizes = (steps, rows, *shapes[0])
    picks = jnp.transpose(row_index, (0, 2, 1, 3))
    sources = [invert(hop_order[visit_index]) for visit_index in range(visits)]
    weights, kept, batch = first_visit(features, targets, picks, model, sizes, slots)
    for visit_index in range(visits):
        weights, moments = move(
            weights, me, batch, kept, sources[visit_index], devices, sizes, slots
        )
        if visit_index + 1 < visits:
            batch = fetch(features, targets, picks, visit_index + 1)
        if visit_index + 1 < visits:
            weights, kept = later_visit(me, batch, weights, moments, sizes, slots)
    results = settle(me, weights, moments, slots, outs)
    return tuple(member[None] for member in results)


def solution(mesh):
    split = P(("groups", "hop"), None, None)
    in_specs = (
        P(("groups", "hop"), None),
        P(("groups", "hop"), None),
        P(("groups", "hop"), None, None, None),
        P("groups", None),
        split,
        split,
        split,
        split,
    )
    return jax.shard_map(
        on_device, mesh=mesh, in_specs=in_specs, out_specs=(split,) * 4, check_vma=False
    )
```

```python
import functools

import jax
import jax.numpy as jnp
from jax import lax
from jax.experimental import pallas as pl
from jax.experimental.pallas import tpu as pltpu
from jax.sharding import PartitionSpec as P


MOMENTUM = 0.9
LEARN_RATE = 0.1
SUB, LANE = 8, 128
MIB = 1 << 20
STRIDE = SUB + 1
FETCH_BLOCKS = 4
FIRST_MIB, FETCH_MIB, LATER_MIB, LAST_MIB, SETTLE_MIB = 58, 58, 58, 58, 16
F32, BF16 = jnp.float32, jnp.bfloat16
HALF_ROOT = 0.7071067811865476
PDF_SCALE = 0.3989422804014327


def table_copies(x_ref, y_ref, held, sems):
    count = x_ref.shape[0]
    block = count // FETCH_BLOCKS
    copies = []
    for part in range(FETCH_BLOCKS):
        place = pl.ds(part * block, block)
        for side, ref in enumerate((x_ref, y_ref)):
            copies.append(
                pltpu.make_async_copy(ref.at[place], held.at[side, place], sems.at[2 * part + side])
            )
    return copies


def build_table(copies, held, table):
    _, count, width = held.shape
    block, lanes = count // FETCH_BLOCKS, width // LANE
    for part in range(FETCH_BLOCKS):
        for side in range(2):
            copies[2 * part + side].wait()
            for lane in range(lanes):
                place = pl.ds(part * block * STRIDE + side * lanes + lane, block, stride=STRIDE)
                table[place, :] = held[
                    side, part * block : (part + 1) * block, lane * LANE : (lane + 1) * LANE
                ].astype(F32)


def pick_rows(picks_ref, step, visit_index, table, picked, outs, first):
    _, groups, _, group_rows = picks_ref.shape
    rows = groups * group_rows

    @pl.loop(0, groups)
    def _(group):
        for offset in range(group_rows):
            pick = picks_ref[step, group, visit_index, offset]
            row = group * group_rows + offset
            picked[pl.ds(row * STRIDE, SUB), :] = table[pl.ds(pick * STRIDE, SUB), :]

    lanes = outs[0].shape[1] // LANE
    for side, ref in enumerate(outs):
        for lane in range(lanes):
            place = pl.ds(side * lanes + lane, rows, stride=STRIDE)
            ref[first : first + rows, lane * LANE : (lane + 1) * LANE] = picked[place, :].astype(
                ref.dtype
            )


def table_scratch(features, rows):
    count, width = features.shape
    if 2 * width > SUB * LANE or count % FETCH_BLOCKS or rows % LANE:
        raise ValueError("sizes")
    return [
        pltpu.VMEM((2, count, width), features.dtype),
        pltpu.VMEM((count * STRIDE, LANE), F32),
        pltpu.VMEM((rows * STRIDE, LANE), F32),
        pltpu.SemaphoreType.DMA((2 * FETCH_BLOCKS,)),
    ]


def fetch_kernel(visit_index, picks_ref, x_ref, y_ref, x_out, y_out, held, table, picked, sems):
    steps, groups, _, group_rows = picks_ref.shape
    rows = groups * group_rows
    copies = table_copies(x_ref, y_ref, held, sems)
    for copy in copies:
        copy.start()
    build_table(copies, held, table)
    for step in range(steps):
        pick_rows(picks_ref, step, visit_index, table, picked, (x_out, y_out), step * rows)


def fetch(features, targets, picks, visit_index):
    count, width = features.shape
    steps, rows = picks.shape[0], picks.shape[1] * picks.shape[3]
    return pl.pallas_call(
        functools.partial(fetch_kernel, visit_index),
        in_specs=[SCALARS, ANYWHERE, ANYWHERE],
        out_specs=[pl.BlockSpec(memory_space=pltpu.VMEM)] * 2,
        out_shape=[jax.ShapeDtypeStruct((steps * rows, width), features.dtype)] * 2,
        scratch_shapes=table_scratch(features, rows),
        compiler_params=pltpu.CompilerParams(vmem_limit_bytes=FETCH_MIB * MIB),
        cost_estimate=pl.CostEstimate(
            flops=0, bytes_accessed=4 * count * width, transcendentals=0
        ),
        name="fetch",
    )(picks, features, targets)


def tiles_of(shape):
    rows, cols = shape[-2:]
    return [
        (row * SUB, col * LANE) for row in range(rows // SUB) for col in range(cols // LANE)
    ]


def tile_slots(shapes, devices):
    slots, base = [], 0
    for shape in shapes:
        tiles = tiles_of(shape)
        if len(tiles) % devices:
            raise ValueError("uneven tiles")
        each = len(tiles) // devices
        slots.append(
            [(index // each, base + index % each, *tile) for index, tile in enumerate(tiles)]
        )
        base += each
    return slots, base


def pack(refs, slots, packed_ref):
    for ref, places in zip(refs, slots):
        for chunk, slot, row, col in places:
            packed_ref[chunk, slot] = ref[row : row + SUB, col : col + LANE].astype(
                packed_ref.dtype
            )


def unpack(packed_ref, slots, refs):
    for ref, places in zip(refs, slots):
        for chunk, slot, row, col in places:
            ref[row : row + SUB, col : col + LANE] = packed_ref[chunk, slot].astype(ref.dtype)


def collect(me_ref, piece_refs, packed_ref, sems):
    chip = me_ref[0] // 2
    return [
        pltpu.make_async_copy(ref, packed_ref.at[chip ^ k], sems.at[k])
        for k, ref in enumerate(piece_refs)
    ]


def scatter(me_ref, packed_ref, piece_refs, sems):
    chip = me_ref[0] // 2
    return [
        pltpu.make_async_copy(packed_ref.at[chip ^ k], ref, sems.at[k])
        for k, ref in enumerate(piece_refs)
    ]


def gradients(x_ref, y_ref, cast_in, cast_out, hid, dout, dpre, block):
    rows = x_ref.shape[0]
    for start in range(0, rows, block):
        part = slice(start, start + block)
        batch_x = x_ref[part, :]
        preact = jnp.dot(batch_x, cast_in, preferred_element_type=F32)
        cdf = 0.5 * (1.0 + lax.erf(preact * HALF_ROOT))
        pdf = PDF_SCALE * jnp.exp(-0.5 * preact * preact)
        hidden = (preact * cdf).astype(BF16)
        hid[part, :] = hidden
        error = (
            batch_x.astype(F32)
            + jnp.dot(hidden, cast_out, preferred_element_type=F32)
            - y_ref[part, :].astype(F32)
        )
        d_out = (error * (1.0 / rows)).astype(BF16)
        dout[part, :] = d_out
        d_hidden = lax.dot_general(
            d_out, cast_out, (((1,), (1,)), ((), ())), preferred_element_type=F32
        )
        dpre[part, :] = (d_hidden * (cdf + preact * pdf)).astype(BF16)


OVER_ROWS = (((0,), (0,)), ((), ()))


def momentum_in(x_ref, dpre, moment):
    grad = lax.dot_general(x_ref[...], dpre[...], OVER_ROWS, preferred_element_type=F32)
    return (MOMENTUM * moment[...].astype(F32) + grad).astype(BF16)


def momentum_out(hid, dout, moment):
    grad = lax.dot_general(hid[...], dout[...], OVER_ROWS, preferred_element_type=F32)
    return (MOMENTUM * moment[...].astype(F32) + grad).astype(BF16)


def stepped(weight, moment):
    return weight - LEARN_RATE * moment.astype(F32)


def train_step(x_ref, y_ref, win, wout, min_, mout, hid, dout, dpre, block):
    cast_in, cast_out = win[...].astype(BF16), wout[...].astype(BF16)
    gradients(x_ref, y_ref, cast_in, cast_out, hid, dout, dpre, block)
    moment = momentum_out(hid, dout, mout)
    mout[...] = moment
    wout[...] = stepped(wout[...], moment)
    moment = momentum_in(x_ref, dpre, min_)
    min_[...] = moment
    win[...] = stepped(win[...], moment)


def hand_over(slots, pieces, state, sent):
    packed, kept = sent[0], sent[1:5]
    pack(state[:2], slots[2 * pieces], packed)
    for ref, held in zip(kept, state):
        ref[...] = held[...].astype(BF16)


def later_visit_kernel(slots, pieces, block, me_ref, x_ref, y_ref, weights_ref, *refs):
    moment_refs, sent, scratch = refs[:pieces], refs[pieces:][:5], refs[pieces + 5 :]
    state, work, (packed, sems) = scratch[:4], scratch[4:7], scratch[7:9]
    step = pl.program_id(0)

    @pl.when(step == 0)
    def _():
        copies = collect(me_ref, moment_refs, packed, sems)
        for copy in copies:
            copy.start()
        unpack(weights_ref, slots[2 * pieces], state[:2])
        for copy in copies:
            copy.wait()
        unpack(packed, slots[pieces], state[2:])
        for weight, moment in zip(state[:2], state[2:]):
            weight[...] = stepped(weight[...], moment[...])

    train_step(x_ref, y_ref, *state, *work, block)

    @pl.when(step == pl.num_programs(0) - 1)
    def _():
        hand_over(slots, pieces, state, sent)


def first_visit_kernel(slots, pieces, block, picks_ref, x_ref, y_ref, *refs):
    model, sent, scratch = refs[:4], refs[4:11], refs[11:]
    state, work, batch = scratch[:4], scratch[4:7], scratch[7:9]
    held, table, picked, sems, model_sems = scratch[9:]
    step = pl.program_id(0)

    @pl.when(step == 0)
    def _():
        copies = table_copies(x_ref, y_ref, held, sems)
        loads = [
            pltpu.make_async_copy(ref, kept, model_sems.at[index])
            for index, (ref, kept) in enumerate(zip(model, state))
        ]
        for copy in copies + loads:
            copy.start()
        build_table(copies, held, table)
        for copy in loads:
            copy.wait()

    pick_rows(picks_ref, step, 0, table, picked, batch, 0)
    train_step(*batch, *state, *work, block)

    @pl.when(step == pl.num_programs(0) - 1)
    def _():
        hand_over(slots, pieces, state, sent)
        pick_rows(picks_ref, step + 1, 0, table, picked, sent[5:], 0)


def last_step_kernel(slots, pieces, block, me_ref, x_ref, y_ref, *refs):
    cast_in, cast_out, min_, mout = refs[:4]
    moment_refs, (hid, dout, dpre, new_in, new_out, packed, sems) = refs[4:-7], refs[-7:]
    gradients(x_ref, y_ref, cast_in[...], cast_out[...], hid, dout, dpre, block)
    new_out[...] = momentum_out(hid, dout, mout)
    new_in[...] = momentum_in(x_ref, dpre, min_)
    pack((new_in, new_out), slots[pieces], packed)
    copies = scatter(me_ref, packed, moment_refs, sems)
    for copy in copies:
        copy.start()
    for copy in copies:
        copy.wait()


def whole(shape):
    return pl.BlockSpec(shape, lambda step: (0,) * len(shape))


SCALARS = pl.BlockSpec(memory_space=pltpu.SMEM)
ANYWHERE = pl.BlockSpec(memory_space=pl.ANY)


def work_scratch(rows, width, hidden):
    return [
        pltpu.VMEM((rows, hidden), BF16),
        pltpu.VMEM((rows, width), BF16),
        pltpu.VMEM((rows, hidden), BF16),
    ]


def step_cost(steps, rows, width, hidden):
    return pl.CostEstimate(
        flops=steps * 10 * rows * width * hidden,
        bytes_accessed=4 * steps * rows * width + 16 * width * hidden,
        transcendentals=2 * steps * rows * hidden,
    )


def visit(kernel, args, in_specs, more_outs, more_scratch, limit, sizes, slots):
    steps, rows, width, hidden = sizes
    pieces = min(slots)
    depth = 2 * width * hidden // (SUB * LANE)
    packed_shape = (2 * pieces, depth // (2 * pieces), SUB, LANE)
    shapes = [packed_shape] + [(width, hidden), (hidden, width)] * 2 + more_outs
    return pl.pallas_call(
        functools.partial(kernel, slots, pieces, rows),
        grid=(steps - 1,),
        in_specs=in_specs,
        out_specs=[whole(shape) for shape in shapes],
        out_shape=[jax.ShapeDtypeStruct(shape, BF16) for shape in shapes],
        scratch_shapes=[
            pltpu.VMEM((width, hidden), F32),
            pltpu.VMEM((hidden, width), F32),
            pltpu.VMEM((width, hidden), BF16),
            pltpu.VMEM((hidden, width), BF16),
            *work_scratch(rows, width, hidden),
            *more_scratch,
        ],
        cost_estimate=step_cost(steps - 1, rows, width, hidden),
        compiler_params=pltpu.CompilerParams(vmem_limit_bytes=limit * MIB),
        name="visit",
    )(*args)


def first_visit(features, targets, picks, model, sizes, slots):
    _, rows, width, _ = sizes
    scratch = [pltpu.VMEM((rows, width), BF16)] * 2 + table_scratch(features, rows)
    outs = visit(
        first_visit_kernel,
        (picks, features, targets, *model),
        [SCALARS] + [ANYWHERE] * 6,
        [(rows, width)] * 2,
        scratch + [pltpu.SemaphoreType.DMA((4,))],
        FIRST_MIB,
        sizes,
        slots,
    )
    return outs[0], outs[1:5], outs[5:]


def piece_scratch(pieces, piece_shape):
    return [pltpu.VMEM((pieces, *piece_shape), BF16), pltpu.SemaphoreType.DMA((pieces,))]


def later_visit(me, batch, weights, moments, sizes, slots):
    _, rows, width, _ = sizes
    batch_spec = pl.BlockSpec((rows, width), lambda step: (step, 0))
    outs = visit(
        later_visit_kernel,
        (me, *batch, weights, *moments),
        [SCALARS, batch_spec, batch_spec, whole(weights.shape)] + [ANYWHERE] * len(moments),
        [],
        piece_scratch(len(moments), moments[0].shape),
        LATER_MIB,
        sizes,
        slots,
    )
    return outs[0], outs[1:]


def last_step(me, batch, kept, sizes, slots):
    _, rows, width, hidden = sizes
    pieces = min(slots)
    piece_shape = (2 * width * hidden // (SUB * LANE) // pieces, SUB, LANE)
    last = batch[0].shape[0] // rows - 1
    batch_spec = pl.BlockSpec((rows, width), lambda step: (last, 0))
    return pl.pallas_call(
        functools.partial(last_step_kernel, slots, pieces, rows),
        grid=(1,),
        in_specs=[SCALARS, batch_spec, batch_spec] + [whole(part.shape) for part in kept],
        out_specs=[ANYWHERE] * pieces,
        out_shape=[jax.ShapeDtypeStruct(piece_shape, BF16)] * pieces,
        scratch_shapes=[
            *work_scratch(rows, width, hidden),
            pltpu.VMEM((width, hidden), BF16),
            pltpu.VMEM((hidden, width), BF16),
            *piece_scratch(pieces, piece_shape),
        ],
        cost_estimate=step_cost(1, rows, width, hidden),
        compiler_params=pltpu.CompilerParams(vmem_limit_bytes=LAST_MIB * MIB),
        name="last",
    )(me, *batch, *kept)


def reorder_kernel(source_ref, packed_ref, out_ref, sems):
    copies = [
        pltpu.make_async_copy(packed_ref.at[source_ref[slot]], out_ref.at[slot], sems.at[slot])
        for slot in range(out_ref.shape[0])
    ]
    for copy in copies:
        copy.start()
    for copy in copies:
        copy.wait()


def reorder(packed, source):
    return pl.pallas_call(
        reorder_kernel,
        in_specs=[
            pl.BlockSpec(memory_space=pltpu.SMEM),
            pl.BlockSpec(memory_space=pltpu.VMEM),
        ],
        out_specs=pl.BlockSpec(memory_space=pl.ANY),
        out_shape=jax.ShapeDtypeStruct(packed.shape, packed.dtype),
        scratch_shapes=[pltpu.SemaphoreType.DMA((packed.shape[0],))],
        compiler_params=pltpu.CompilerParams(vmem_limit_bytes=8 * MIB),
        name="reorder",
    )(source, packed)


def stack_kernel(*refs):
    parts, out_ref, sems = refs[:-2], refs[-2], refs[-1]
    copies = [
        pltpu.make_async_copy(ref, out_ref.at[k], sems.at[k]) for k, ref in enumerate(parts)
    ]
    for copy in copies:
        copy.start()
    for copy in copies:
        copy.wait()


def stacked(parts):
    shape = (len(parts), *parts[0].shape)
    return pl.pallas_call(
        stack_kernel,
        in_specs=[ANYWHERE] * len(parts),
        out_specs=pl.BlockSpec(memory_space=pltpu.VMEM),
        out_shape=jax.ShapeDtypeStruct(shape, parts[0].dtype),
        scratch_shapes=[pltpu.SemaphoreType.DMA((len(parts),))],
        compiler_params=pltpu.CompilerParams(vmem_limit_bytes=8 * MIB),
        name="stack",
    )(*parts)


def route_kernel(pieces, me_ref, source_ref, own_ref, partner_ref, *refs):
    out_refs, sems = refs[:pieces], refs[pieces]
    chip, core = me_ref[0] // 2, me_ref[0] % 2
    for k, out_ref in enumerate(out_refs):
        source = source_ref[2 * (chip ^ k) + core]
        place = chip ^ (source // 2)

        @pl.when(source % 2 == core)
        def _():
            pltpu.make_async_copy(own_ref.at[place], out_ref, sems.at[k]).start()

        @pl.when(source % 2 != core)
        def _():
            pltpu.make_async_copy(partner_ref.at[place], out_ref, sems.at[k]).start()

    for k, out_ref in enumerate(out_refs):
        pltpu.make_async_copy(own_ref.at[0], out_ref, sems.at[k]).wait()


def route(me, source, own, partner):
    pieces = own.shape[0]
    in_vmem = pl.BlockSpec(memory_space=pltpu.VMEM)
    return pl.pallas_call(
        functools.partial(route_kernel, pieces),
        in_specs=[SCALARS, SCALARS, in_vmem, in_vmem],
        out_specs=[ANYWHERE] * pieces,
        out_shape=[jax.ShapeDtypeStruct(own.shape[1:], own.dtype)] * pieces,
        scratch_shapes=[pltpu.SemaphoreType.DMA((pieces,))],
        cost_estimate=pl.CostEstimate(
            flops=0, bytes_accessed=4 * own.size, transcendentals=0
        ),
        compiler_params=pltpu.CompilerParams(vmem_limit_bytes=8 * MIB),
        name="route",
    )(me, source, own, partner)


def settle_kernel(slots, pieces, me_ref, weights_ref, *refs):
    moment_refs, outs, (packed, sems) = refs[:pieces], refs[pieces:-2], refs[-2:]
    copies = collect(me_ref, moment_refs, packed, sems)
    for copy in copies:
        copy.start()
    unpack(weights_ref, slots[2 * pieces], outs[:2])
    for copy in copies:
        copy.wait()
    unpack(packed, slots[pieces], outs[2:])
    for weight, moment in zip(outs[:2], outs[2:]):
        weight[...] = stepped(weight[...], moment[...])


def settle(me, weights, moments, slots, outs):
    in_vmem = pl.BlockSpec(memory_space=pltpu.VMEM)
    return pl.pallas_call(
        functools.partial(settle_kernel, slots, len(moments)),
        in_specs=[SCALARS, in_vmem] + [ANYWHERE] * len(moments),
        out_specs=[in_vmem] * len(outs),
        out_shape=[jax.ShapeDtypeStruct(shape, dtype) for shape, dtype in outs],
        scratch_shapes=piece_scratch(len(moments), moments[0].shape),
        compiler_params=pltpu.CompilerParams(vmem_limit_bytes=SETTLE_MIB * MIB),
        name="settle",
    )(me, weights, *moments)


def invert(order):
    count = order.shape[0]
    places = jnp.arange(count, dtype=jnp.int32)
    matches = order[:, None] == places[None, :]
    return jnp.sum(jnp.where(matches, places[:, None], 0), axis=0).astype(jnp.int32)


def exchange(packed):
    return lax.all_to_all(packed, "hop", split_axis=0, concat_axis=0, tiled=True)


def spread(parts, devices):
    moved = [None] * len(parts)
    moved[0] = parts[0]
    for k in sorted(range(1, len(parts)), reverse=True):
        moved[k] = lax.ppermute(parts[k], "hop", [(i, i ^ (2 * k)) for i in range(devices)])
    return moved


def move(weights, me, batch, kept, source, devices, sizes, slots):
    weights = exchange(weights)
    moments = last_step(me, batch, kept, sizes, slots)
    moments = spread(moments, devices)
    weights = reorder(weights, source)
    weights = exchange(weights)
    own = stacked(moments)
    partner = lax.ppermute(own, "hop", [(i, i ^ 1) for i in range(devices)])
    moments = route(me, source, own, partner)
    moments = spread(moments, devices)
    return weights, moments


def on_device(
    features, targets, row_index, hop_order, weight_in, weight_out, moment_in, moment_out
):
    devices = lax.axis_size("hop")
    me = lax.axis_index("hop").astype(jnp.int32).reshape(1)
    model = (weight_in[0], weight_out[0], moment_in[0], moment_out[0])
    outs = [(member.shape, member.dtype) for member in model]
    shapes = [member.shape for member in model[:2]]
    slots = {count: tile_slots(shapes, count)[0] for count in (devices // 2, devices)}
    _, visits, steps, rows = row_index.shape
    sizes = (steps, rows, *shapes[0])
    picks = row_index.reshape(visits, steps, rows // LANE, LANE).transpose(1, 2, 0, 3)
    sources = [invert(hop_order[visit_index]) for visit_index in range(visits)]
    weights, kept, batch = first_visit(features, targets, picks, model, sizes, slots)
    for visit_index in range(visits):
        weights, moments = move(
            weights, me, batch, kept, sources[visit_index], devices, sizes, slots
        )
        if visit_index + 1 < visits:
            batch = fetch(features, targets, picks, visit_index + 1)
        if visit_index + 1 < visits:
            weights, kept = later_visit(me, batch, weights, moments, sizes, slots)
    results = settle(me, weights, moments, slots, outs)
    return tuple(member[None] for member in results)


def solution(mesh):
    split = P(("groups", "hop"), None, None)
    in_specs = (
        P(("groups", "hop"), None),
        P(("groups", "hop"), None),
        P(("groups", "hop"), None, None, None),
        P("groups", None),
        split,
        split,
        split,
        split,
    )
    return jax.shard_map(
        on_device, mesh=mesh, in_specs=in_specs, out_specs=(split,) * 4, check_vma=False
    )
```

```python
import functools

import jax
import jax.numpy as jnp
from jax import lax
from jax.experimental import pallas as pl
from jax.experimental.pallas import tpu as pltpu
from jax.sharding import PartitionSpec as P


MOMENTUM = 0.9
LEARN_RATE = 0.1
SUB, LANE = 8, 128
MIB = 1 << 20
STRIDE = SUB + 1
FETCH_BLOCKS = 4
FIRST_MIB, FETCH_MIB, LATER_MIB, LAST_MIB, SETTLE_MIB = 58, 58, 53, 58, 16
F32, BF16 = jnp.float32, jnp.bfloat16
HALF_ROOT = 0.7071067811865476
PDF_SCALE = 0.3989422804014327


def table_copies(x_ref, y_ref, held, sems):
    count = x_ref.shape[0]
    block = count // FETCH_BLOCKS
    copies = []
    for part in range(FETCH_BLOCKS):
        place = pl.ds(part * block, block)
        for side, ref in enumerate((x_ref, y_ref)):
            copies.append(
                pltpu.make_async_copy(ref.at[place], held.at[side, place], sems.at[2 * part + side])
            )
    return copies


def build_table(copies, held, table):
    _, count, width = held.shape
    block, lanes = count // FETCH_BLOCKS, width // LANE
    for part in range(FETCH_BLOCKS):
        for side in range(2):
            copies[2 * part + side].wait()
            for lane in range(lanes):
                place = pl.ds(part * block * STRIDE + side * lanes + lane, block, stride=STRIDE)
                table[place, :] = held[
                    side, part * block : (part + 1) * block, lane * LANE : (lane + 1) * LANE
                ].astype(F32)


def pick_rows(picks_ref, step, visit_index, table, picked, outs, first):
    _, groups, _, group_rows = picks_ref.shape
    rows = groups * group_rows

    @pl.loop(0, groups)
    def _(group):
        for offset in range(group_rows):
            pick = picks_ref[step, group, visit_index, offset]
            row = group * group_rows + offset
            picked[pl.ds(row * STRIDE, SUB), :] = table[pl.ds(pick * STRIDE, SUB), :]

    lanes = outs[0].shape[1] // LANE
    for side, ref in enumerate(outs):
        for lane in range(lanes):
            place = pl.ds(side * lanes + lane, rows, stride=STRIDE)
            ref[first : first + rows, lane * LANE : (lane + 1) * LANE] = picked[place, :].astype(
                ref.dtype
            )


def table_scratch(features, rows):
    count, width = features.shape
    if 2 * width > SUB * LANE or count % FETCH_BLOCKS or rows % LANE:
        raise ValueError("sizes")
    return [
        pltpu.VMEM((2, count, width), features.dtype),
        pltpu.VMEM((count * STRIDE, LANE), F32),
        pltpu.VMEM((rows * STRIDE, LANE), F32),
        pltpu.SemaphoreType.DMA((2 * FETCH_BLOCKS,)),
    ]


def fetch_kernel(visit_index, picks_ref, x_ref, y_ref, x_out, y_out, held, table, picked, sems):
    steps, groups, _, group_rows = picks_ref.shape
    rows = groups * group_rows
    copies = table_copies(x_ref, y_ref, held, sems)
    for copy in copies:
        copy.start()
    build_table(copies, held, table)
    for step in range(steps):
        pick_rows(picks_ref, step, visit_index, table, picked, (x_out, y_out), step * rows)


def fetch(features, targets, picks, visit_index):
    count, width = features.shape
    steps, rows = picks.shape[0], picks.shape[1] * picks.shape[3]
    return pl.pallas_call(
        functools.partial(fetch_kernel, visit_index),
        in_specs=[SCALARS, ANYWHERE, ANYWHERE],
        out_specs=[pl.BlockSpec(memory_space=pltpu.VMEM)] * 2,
        out_shape=[jax.ShapeDtypeStruct((steps * rows, width), features.dtype)] * 2,
        scratch_shapes=table_scratch(features, rows),
        compiler_params=pltpu.CompilerParams(vmem_limit_bytes=FETCH_MIB * MIB),
        cost_estimate=pl.CostEstimate(
            flops=0, bytes_accessed=4 * count * width, transcendentals=0
        ),
        name="fetch",
    )(picks, features, targets)


def tiles_of(shape):
    rows, cols = shape[-2:]
    return [
        (row * SUB, col * LANE) for row in range(rows // SUB) for col in range(cols // LANE)
    ]


def tile_slots(shapes, devices):
    slots, base = [], 0
    for shape in shapes:
        tiles = tiles_of(shape)
        if len(tiles) % devices:
            raise ValueError("uneven tiles")
        each = len(tiles) // devices
        slots.append(
            [(index // each, base + index % each, *tile) for index, tile in enumerate(tiles)]
        )
        base += each
    return slots, base


def pack(refs, slots, packed_ref):
    for ref, places in zip(refs, slots):
        for chunk, slot, row, col in places:
            packed_ref[chunk, slot] = ref[row : row + SUB, col : col + LANE].astype(
                packed_ref.dtype
            )


def unpack(packed_ref, slots, refs):
    for ref, places in zip(refs, slots):
        for chunk, slot, row, col in places:
            ref[row : row + SUB, col : col + LANE] = packed_ref[chunk, slot].astype(ref.dtype)


def collect(me_ref, piece_refs, packed_ref, sems):
    chip = me_ref[0] // 2
    return [
        pltpu.make_async_copy(ref, packed_ref.at[chip ^ k], sems.at[k])
        for k, ref in enumerate(piece_refs)
    ]


def scatter(me_ref, packed_ref, piece_refs, sems):
    chip = me_ref[0] // 2
    return [
        pltpu.make_async_copy(packed_ref.at[chip ^ k], ref, sems.at[k])
        for k, ref in enumerate(piece_refs)
    ]


def gradients(x_ref, y_ref, cast_in, cast_out, hid, dout, dpre, block):
    rows = x_ref.shape[0]
    for start in range(0, rows, block):
        part = slice(start, start + block)
        batch_x = x_ref[part, :]
        preact = jnp.dot(batch_x, cast_in, preferred_element_type=F32)
        cdf = 0.5 * (1.0 + lax.erf(preact * HALF_ROOT))
        pdf = PDF_SCALE * jnp.exp(-0.5 * preact * preact)
        hidden = (preact * cdf).astype(BF16)
        hid[part, :] = hidden
        error = (
            batch_x.astype(F32)
            + jnp.dot(hidden, cast_out, preferred_element_type=F32)
            - y_ref[part, :].astype(F32)
        )
        d_out = (error * (1.0 / rows)).astype(BF16)
        dout[part, :] = d_out
        d_hidden = lax.dot_general(
            d_out, cast_out, (((1,), (1,)), ((), ())), preferred_element_type=F32
        )
        dpre[part, :] = (d_hidden * (cdf + preact * pdf)).astype(BF16)


OVER_ROWS = (((0,), (0,)), ((), ()))


def momentum_in(x_ref, dpre, moment):
    grad = lax.dot_general(x_ref[...], dpre[...], OVER_ROWS, preferred_element_type=F32)
    return (MOMENTUM * moment[...].astype(F32) + grad).astype(BF16)


def momentum_out(hid, dout, moment):
    grad = lax.dot_general(hid[...], dout[...], OVER_ROWS, preferred_element_type=F32)
    return (MOMENTUM * moment[...].astype(F32) + grad).astype(BF16)


def stepped(weight, moment):
    return weight - LEARN_RATE * moment.astype(F32)


def train_step(x_ref, y_ref, win, wout, min_, mout, hid, dout, dpre, block):
    cast_in, cast_out = win[...].astype(BF16), wout[...].astype(BF16)
    gradients(x_ref, y_ref, cast_in, cast_out, hid, dout, dpre, block)
    moment = momentum_out(hid, dout, mout)
    mout[...] = moment
    wout[...] = stepped(wout[...], moment)
    moment = momentum_in(x_ref, dpre, min_)
    min_[...] = moment
    win[...] = stepped(win[...], moment)


def hand_over(slots, pieces, state, sent):
    pack(state[:2], slots[2 * pieces], sent[0])
    for ref, held in zip(sent[1:3], state[2:]):
        ref[...] = held[...]


def later_visit_kernel(slots, pieces, block, me_ref, x_ref, y_ref, weights_ref, *refs):
    moment_refs, sent, scratch = refs[:pieces], refs[pieces:][:3], refs[pieces + 3 :]
    state, work, (packed, sems, packed_weights, sem) = scratch[:4], scratch[4:7], scratch[7:]
    step = pl.program_id(0)

    @pl.when(step == 0)
    def _():
        load = pltpu.make_async_copy(weights_ref, packed_weights, sem)
        load.start()
        copies = collect(me_ref, moment_refs, packed, sems)
        for copy in copies:
            copy.start()
        load.wait()
        unpack(packed_weights, slots[2 * pieces], state[:2])
        for copy in copies:
            copy.wait()
        unpack(packed, slots[pieces], state[2:])
        for weight, moment in zip(state[:2], state[2:]):
            weight[...] = stepped(weight[...], moment[...])

    train_step(x_ref, y_ref, *state, *work, block)

    @pl.when(step == pl.num_programs(0) - 1)
    def _():
        hand_over(slots, pieces, state, sent)


def first_visit_kernel(slots, pieces, block, picks_ref, x_ref, y_ref, *refs):
    model, sent, scratch = refs[:4], refs[4:9], refs[9:]
    state, work, batch = scratch[:4], scratch[4:7], scratch[7:9]
    held, table, picked, sems, model_sems = scratch[9:]
    step = pl.program_id(0)

    @pl.when(step == 0)
    def _():
        copies = table_copies(x_ref, y_ref, held, sems)
        loads = [
            pltpu.make_async_copy(ref, kept, model_sems.at[index])
            for index, (ref, kept) in enumerate(zip(model, state))
        ]
        for copy in copies + loads:
            copy.start()
        build_table(copies, held, table)
        for copy in loads:
            copy.wait()

    pick_rows(picks_ref, step, 0, table, picked, batch, 0)
    train_step(*batch, *state, *work, block)

    @pl.when(step == pl.num_programs(0) - 1)
    def _():
        hand_over(slots, pieces, state, sent)
        pick_rows(picks_ref, step + 1, 0, table, picked, sent[3:], 0)


def last_step_kernel(slots, pieces, block, me_ref, x_ref, y_ref, *refs):
    weights_ref, min_, mout = refs[:3]
    moment_refs, (hid, dout, dpre, new_in, new_out, packed, sems) = refs[3:-9], refs[-9:-2]
    cast_in, cast_out = refs[-2:]
    unpack(weights_ref, slots[2 * pieces], (cast_in, cast_out))
    gradients(x_ref, y_ref, cast_in[...], cast_out[...], hid, dout, dpre, block)
    new_out[...] = momentum_out(hid, dout, mout)
    new_in[...] = momentum_in(x_ref, dpre, min_)
    pack((new_in, new_out), slots[pieces], packed)
    copies = scatter(me_ref, packed, moment_refs, sems)
    for copy in copies:
        copy.start()
    for copy in copies:
        copy.wait()


def whole(shape):
    return pl.BlockSpec(shape, lambda step: (0,) * len(shape))


SCALARS = pl.BlockSpec(memory_space=pltpu.SMEM)
ANYWHERE = pl.BlockSpec(memory_space=pl.ANY)


def work_scratch(rows, width, hidden):
    return [
        pltpu.VMEM((rows, hidden), BF16),
        pltpu.VMEM((rows, width), BF16),
        pltpu.VMEM((rows, hidden), BF16),
    ]


def step_cost(steps, rows, width, hidden):
    return pl.CostEstimate(
        flops=steps * 10 * rows * width * hidden,
        bytes_accessed=4 * steps * rows * width + 16 * width * hidden,
        transcendentals=2 * steps * rows * hidden,
    )


def visit(kernel, args, in_specs, more_outs, more_scratch, limit, sizes, slots):
    steps, rows, width, hidden = sizes
    pieces = min(slots)
    depth = 2 * width * hidden // (SUB * LANE)
    packed_shape = (2 * pieces, depth // (2 * pieces), SUB, LANE)
    shapes = [packed_shape, (width, hidden), (hidden, width)] + more_outs
    return pl.pallas_call(
        functools.partial(kernel, slots, pieces, rows),
        grid=(steps - 1,),
        in_specs=in_specs,
        out_specs=[whole(shape) for shape in shapes],
        out_shape=[jax.ShapeDtypeStruct(shape, BF16) for shape in shapes],
        scratch_shapes=[
            pltpu.VMEM((width, hidden), F32),
            pltpu.VMEM((hidden, width), F32),
            pltpu.VMEM((width, hidden), BF16),
            pltpu.VMEM((hidden, width), BF16),
            *work_scratch(rows, width, hidden),
            *more_scratch,
        ],
        cost_estimate=step_cost(steps - 1, rows, width, hidden),
        compiler_params=pltpu.CompilerParams(vmem_limit_bytes=limit * MIB),
        name="visit",
    )(*args)


def first_visit(features, targets, picks, model, sizes, slots):
    _, rows, width, _ = sizes
    scratch = [pltpu.VMEM((rows, width), BF16)] * 2 + table_scratch(features, rows)
    outs = visit(
        first_visit_kernel,
        (picks, features, targets, *model),
        [SCALARS] + [ANYWHERE] * 6,
        [(rows, width)] * 2,
        scratch + [pltpu.SemaphoreType.DMA((4,))],
        FIRST_MIB,
        sizes,
        slots,
    )
    return outs[0], outs[1:3], outs[3:]


def piece_scratch(pieces, piece_shape):
    return [pltpu.VMEM((pieces, *piece_shape), BF16), pltpu.SemaphoreType.DMA((pieces,))]


def later_visit(me, batch, weights, moments, sizes, slots):
    _, rows, width, _ = sizes
    batch_spec = pl.BlockSpec((rows, width), lambda step: (step, 0))
    outs = visit(
        later_visit_kernel,
        (me, *batch, weights, *moments),
        [SCALARS, batch_spec, batch_spec] + [ANYWHERE] * (1 + len(moments)),
        [],
        piece_scratch(len(moments), moments[0].shape)
        + [pltpu.VMEM(weights.shape, BF16), pltpu.SemaphoreType.DMA],
        LATER_MIB,
        sizes,
        slots,
    )
    return outs[0], outs[1:]


def last_step(me, batch, weights, kept, sizes, slots):
    _, rows, width, hidden = sizes
    pieces = min(slots)
    piece_shape = (2 * width * hidden // (SUB * LANE) // pieces, SUB, LANE)
    last = batch[0].shape[0] // rows - 1
    batch_spec = pl.BlockSpec((rows, width), lambda step: (last, 0))
    return pl.pallas_call(
        functools.partial(last_step_kernel, slots, pieces, rows),
        grid=(1,),
        in_specs=[SCALARS, batch_spec, batch_spec] + [whole(part.shape) for part in (weights, *kept)],
        out_specs=[ANYWHERE] * pieces,
        out_shape=[jax.ShapeDtypeStruct(piece_shape, BF16)] * pieces,
        scratch_shapes=[
            *work_scratch(rows, width, hidden),
            pltpu.VMEM((width, hidden), BF16),
            pltpu.VMEM((hidden, width), BF16),
            *piece_scratch(pieces, piece_shape),
            pltpu.VMEM((width, hidden), BF16),
            pltpu.VMEM((hidden, width), BF16),
        ],
        cost_estimate=step_cost(1, rows, width, hidden),
        compiler_params=pltpu.CompilerParams(vmem_limit_bytes=LAST_MIB * MIB),
        name="last",
    )(me, *batch, weights, *kept)


def reorder_kernel(source_ref, packed_ref, out_ref, sems):
    copies = [
        pltpu.make_async_copy(packed_ref.at[source_ref[slot]], out_ref.at[slot], sems.at[slot])
        for slot in range(out_ref.shape[0])
    ]
    for copy in copies:
        copy.start()
    for copy in copies:
        copy.wait()


def reorder(packed, source):
    return pl.pallas_call(
        reorder_kernel,
        in_specs=[
            pl.BlockSpec(memory_space=pltpu.SMEM),
            pl.BlockSpec(memory_space=pltpu.VMEM),
        ],
        out_specs=pl.BlockSpec(memory_space=pl.ANY),
        out_shape=jax.ShapeDtypeStruct(packed.shape, packed.dtype),
        scratch_shapes=[pltpu.SemaphoreType.DMA((packed.shape[0],))],
        compiler_params=pltpu.CompilerParams(vmem_limit_bytes=8 * MIB),
        name="reorder",
    )(source, packed)


def stack_kernel(*refs):
    parts, out_ref, sems = refs[:-2], refs[-2], refs[-1]
    copies = [
        pltpu.make_async_copy(ref, out_ref.at[k], sems.at[k]) for k, ref in enumerate(parts)
    ]
    for copy in copies:
        copy.start()
    for copy in copies:
        copy.wait()


def stacked(parts):
    shape = (len(parts), *parts[0].shape)
    return pl.pallas_call(
        stack_kernel,
        in_specs=[ANYWHERE] * len(parts),
        out_specs=pl.BlockSpec(memory_space=pltpu.VMEM),
        out_shape=jax.ShapeDtypeStruct(shape, parts[0].dtype),
        scratch_shapes=[pltpu.SemaphoreType.DMA((len(parts),))],
        compiler_params=pltpu.CompilerParams(vmem_limit_bytes=8 * MIB),
        name="stack",
    )(*parts)


def route_kernel(pieces, me_ref, source_ref, own_ref, partner_ref, *refs):
    out_refs, sems = refs[:pieces], refs[pieces]
    chip, core = me_ref[0] // 2, me_ref[0] % 2
    for k, out_ref in enumerate(out_refs):
        source = source_ref[2 * (chip ^ k) + core]
        place = chip ^ (source // 2)

        @pl.when(source % 2 == core)
        def _():
            pltpu.make_async_copy(own_ref.at[place], out_ref, sems.at[k]).start()

        @pl.when(source % 2 != core)
        def _():
            pltpu.make_async_copy(partner_ref.at[place], out_ref, sems.at[k]).start()

    for k, out_ref in enumerate(out_refs):
        pltpu.make_async_copy(own_ref.at[0], out_ref, sems.at[k]).wait()


def route(me, source, own, partner):
    pieces = own.shape[0]
    in_vmem = pl.BlockSpec(memory_space=pltpu.VMEM)
    return pl.pallas_call(
        functools.partial(route_kernel, pieces),
        in_specs=[SCALARS, SCALARS, in_vmem, in_vmem],
        out_specs=[ANYWHERE] * pieces,
        out_shape=[jax.ShapeDtypeStruct(own.shape[1:], own.dtype)] * pieces,
        scratch_shapes=[pltpu.SemaphoreType.DMA((pieces,))],
        cost_estimate=pl.CostEstimate(
            flops=0, bytes_accessed=4 * own.size, transcendentals=0
        ),
        compiler_params=pltpu.CompilerParams(vmem_limit_bytes=8 * MIB),
        name="route",
    )(me, source, own, partner)


def settle_kernel(slots, pieces, me_ref, weights_ref, *refs):
    moment_refs, outs, scratch = refs[:pieces], refs[pieces:][:4], refs[pieces + 4 :]
    packed, sems, packed_weights, sem, out_sems = scratch[:5]
    made = scratch[5:]
    load = pltpu.make_async_copy(weights_ref, packed_weights, sem)
    load.start()
    copies = collect(me_ref, moment_refs, packed, sems)
    for copy in copies:
        copy.start()
    stores = [
        pltpu.make_async_copy(ref, out, out_sems.at[index])
        for index, (ref, out) in enumerate(zip(made, outs))
    ]
    load.wait()
    unpack(packed_weights, slots[2 * pieces], made[:2])
    for copy in copies:
        copy.wait()
    unpack(packed, slots[pieces], made[2:])
    for side in range(2):
        stores[2 + side].start()
        made[side][...] = stepped(made[side][...], made[2 + side][...])
        stores[side].start()
    for store in stores:
        store.wait()


def settle(me, weights, moments, slots, outs):
    return pl.pallas_call(
        functools.partial(settle_kernel, slots, len(moments)),
        in_specs=[SCALARS] + [ANYWHERE] * (1 + len(moments)),
        out_specs=[ANYWHERE] * len(outs),
        out_shape=[jax.ShapeDtypeStruct(shape, dtype) for shape, dtype in outs],
        scratch_shapes=piece_scratch(len(moments), moments[0].shape)
        + [pltpu.VMEM(weights.shape, BF16), pltpu.SemaphoreType.DMA]
        + [pltpu.SemaphoreType.DMA((len(outs),))]
        + [pltpu.VMEM(shape, dtype) for shape, dtype in outs],
        compiler_params=pltpu.CompilerParams(vmem_limit_bytes=SETTLE_MIB * MIB),
        name="settle",
    )(me, weights, *moments)


def invert(order):
    count = order.shape[0]
    places = jnp.arange(count, dtype=jnp.int32)
    matches = order[:, None] == places[None, :]
    return jnp.sum(jnp.where(matches, places[:, None], 0), axis=0).astype(jnp.int32)


def exchange(packed):
    return lax.all_to_all(packed, "hop", split_axis=0, concat_axis=0, tiled=True)


def spread(parts, devices):
    moved = [None] * len(parts)
    moved[0] = parts[0]
    for k in sorted(range(1, len(parts)), key=lambda k: (k >= len(parts) // 2, -k)):
        moved[k] = lax.ppermute(parts[k], "hop", [(i, i ^ (2 * k)) for i in range(devices)])
    return moved


def move(weights, me, batch, kept, source, devices, sizes, slots):
    moments = last_step(me, batch, weights, kept, sizes, slots)
    weights = exchange(weights)
    moments = spread(moments, devices)
    weights = reorder(weights, source)
    weights = exchange(weights)
    own = stacked(moments)
    partner = lax.ppermute(own, "hop", [(i, i ^ 1) for i in range(devices)])
    moments = route(me, source, own, partner)
    moments = spread(moments, devices)
    return weights, moments


def on_device(
    features, targets, row_index, hop_order, weight_in, weight_out, moment_in, moment_out
):
    devices = lax.axis_size("hop")
    me = lax.axis_index("hop").astype(jnp.int32).reshape(1)
    model = (weight_in[0], weight_out[0], moment_in[0], moment_out[0])
    outs = [(member.shape, member.dtype) for member in model]
    shapes = [member.shape for member in model[:2]]
    slots = {count: tile_slots(shapes, count)[0] for count in (devices // 2, devices)}
    _, visits, steps, rows = row_index.shape
    sizes = (steps, rows, *shapes[0])
    picks = row_index.reshape(visits, steps, rows // LANE, LANE).transpose(1, 2, 0, 3)
    sources = [invert(hop_order[visit_index]) for visit_index in range(visits)]
    weights, kept, batch = first_visit(features, targets, picks, model, sizes, slots)
    for visit_index in range(visits):
        weights, moments = move(
            weights, me, batch, kept, sources[visit_index], devices, sizes, slots
        )
        if visit_index + 1 < visits:
            batch = fetch(features, targets, picks, visit_index + 1)
        if visit_index + 1 < visits:
            weights, kept = later_visit(me, batch, weights, moments, sizes, slots)
    results = settle(me, weights, moments, slots, outs)
    return tuple(member[None] for member in results)


def solution(mesh):
    split = P(("groups", "hop"), None, None)
    in_specs = (
        P(("groups", "hop"), None),
        P(("groups", "hop"), None),
        P(("groups", "hop"), None, None, None),
        P("groups", None),
        split,
        split,
        split,
        split,
    )
    return jax.shard_map(
        on_device, mesh=mesh, in_specs=in_specs, out_specs=(split,) * 4, check_vma=False
    )
```
